128 devices in a mesh: dp: 32 (over y, x, core), tensor: 4 (over z).
Axes of the slice: x: 4, y: 4, z: 4, core: 2. Of those that a mesh axis runs over, the one named last changes fastest.
Arguments:
- dec_hidden: bfloat16 [26624, 8192], P('dp', 'tensor'), may hold values from -192 to 192
- dec_query: bfloat16 [26624, 4096], P('dp', 'tensor'), may hold values from -448 to 448
- store: bfloat16 [128, 64, 2048], P('dp'), may hold values from -6 to 6
- norm_gain: float32 [2048], replicated, may hold values from 0.25 to 1.75
- w_query_enc: bfloat16 [2048, 1024], P(None, 'tensor'), may hold values from -8 to 8
- w_cond: bfloat16 [8192, 2048], P('tensor'), may hold values from -1 to 1
- w_out_enc: bfloat16 [1024, 2048], P('tensor'), may hold values from -1 to 1
- w_kv_dec: bfloat16 [2048, 8192], P(None, 'tensor'), may hold values from -1 to 1
- owner: int32 [416, 2], P('dp'), may hold values from 0 to 31, all different within a row; in each aligned block of 13 rows (0 to 12, 13 to 25, ...) at most 2 rows name the same one
- nb_index: int32 [416, 2], P('dp'), may hold values from 0 to 3
- nb_count: int32 [416], P('dp'), may hold values from 1 to 2
Outputs:
- cca: bfloat16 [26624, 4096], P('dp', 'tensor')
The draws below stay inside these ranges and needn't reach their ends.
Inputs may be any that keep to these rules, and one draw needn't show every extreme that they name: A span's 2 owners differ; among the 13 spans of one dp index no owner is named by more than 2 spans, a bound that some block reaches.
All inputs are finite; a program needn't handle non-finite values.
Results may differ from the reference program's by a relative error of at most 0.008.
Values may be sent and summed in bfloat16 or wider, within the bound.
A program may use at most 128 MiB of HBM per device.

```python
import math
import jax
import jax.numpy as jnp
import numpy as np
from jax import lax

D = 8192
E = 2048
HEAD = 128
HE = 8
HD = 32
SPAN = 64
NBLEN = 64
KN = 2
CH_DEV = 13
NB_STORE = 4
CAP = 2
SPANS = 416
TOKENS = 26624
STORE_ALL = 128
N_DP = 32


def clipped_normal(key, shape, factor):
    return jnp.clip(jax.random.normal(key, shape, jnp.float32), -6.0, 6.0) * factor


def draw_dec_hidden(key, part):
    sub = jax.random.fold_in(key, 11)
    values = clipped_normal(sub, (TOKENS, D), 1.0)
    return values.astype(jnp.bfloat16)


def draw_dec_query(key, part):
    sub = jax.random.fold_in(key, 12)
    width = HD * HEAD
    values = clipped_normal(sub, (TOKENS, width), 1.0)
    return values.astype(jnp.bfloat16)


def draw_store(key, part):
    sub = jax.random.fold_in(key, 13)
    values = clipped_normal(sub, (STORE_ALL, NBLEN, E), 1.0)
    return values.astype(jnp.bfloat16)


def draw_w_query_enc(key, part):
    sub = jax.random.fold_in(key, 14)
    factor = 1.0 / math.sqrt(E)
    values = clipped_normal(sub, (E, HE * HEAD), factor)
    return values.astype(jnp.bfloat16)


def draw_w_cond(key, part):
    sub = jax.random.fold_in(key, 15)
    factor = 1.0 / math.sqrt(D)
    values = clipped_normal(sub, (D, 2 * HE * HEAD), factor)
    return values.astype(jnp.bfloat16)


def draw_w_out_enc(key, part):
    sub = jax.random.fold_in(key, 16)
    factor = 1.0 / math.sqrt(HE * HEAD)
    values = clipped_normal(sub, (HE * HEAD, E), factor)
    return values.astype(jnp.bfloat16)


def draw_w_kv_dec(key, part):
    sub = jax.random.fold_in(key, 17)
    factor = 1.0 / math.sqrt(E)
    values = clipped_normal(sub, (E, 2 * HD * HEAD), factor)
    return values.astype(jnp.bfloat16)


def with_ends(entries, stream_key, least, high):
    extent = entries.shape
    spot = [jax.random.randint(jax.random.fold_in(stream_key, axis), (), 0, extent[axis]) for axis in range(len(extent))]
    entries = entries.at[tuple(spot)].set(least)
    longest = extent.index(max(extent))
    spot[longest] = (spot[longest] + 1) % extent[longest]
    return entries.at[tuple(spot)].set(high)


def assign_block(own_key, own, number, rows, amount, top, reach, slope):
    ranking = jax.random.permutation(own_key, amount)
    heavy_load, ordinary = shares(amount, rows * top, reach, slope, True), shares(amount, rows * top, reach, slope, False)
    places = jnp.arange(amount)

    def named(lengths, rotation):
        used = int((lengths > 0).sum())
        fixed = max(1, used // 4)
        shifted = fixed + (places - fixed + rotation * (used - fixed)) % max(1, amount - fixed)
        return jnp.zeros((amount,), jnp.int32).at[ranking[jnp.where(places < fixed, places, shifted)]].set(jnp.asarray(lengths, jnp.int32))

    lengths = jnp.where(number % 4 == 0, named(heavy_load, number // 4), named(ordinary, number - number // 4 - 1))
    mixed = jax.random.permutation(jax.random.fold_in(own, 3), amount)
    giver, sink = mixed[0:amount // 2 * 2:2], mixed[1:amount // 2 * 2:2]
    margin = jnp.minimum(lengths[giver] - 1, reach - lengths[sink]) // 2
    margin = jnp.where((giver == ranking[0]) | (sink == ranking[0]) | (lengths[sink] == 0), 0, jnp.maximum(margin, 0))
    shifted = jax.random.randint(jax.random.fold_in(own, 4), (amount // 2,), 0, 1 << 20) % (margin + 1)
    lengths = lengths.at[giver].add(-shifted).at[sink].add(shifted)
    labels = jnp.searchsorted(jnp.cumsum(lengths), jnp.arange(rows * top), side="right").astype(jnp.int32)
    grid = labels.reshape(top, rows).T
    grid = grid[jax.random.permutation(jax.random.fold_in(own, 1), rows)]
    rotation = jax.random.randint(jax.random.fold_in(own, 2), (rows, 1), 0, top)
    return jnp.take_along_axis(grid, (jnp.arange(top)[None, :] + rotation) % top, axis=1)


def shares(count, total, bound, lean, full):
    portions = [(1 << 20) // math.isqrt(standing ** lean) + 1 for standing in range(1, count + 1)]
    largest = bound if full else min(bound, max(-(-total // count), total * portions[0] // sum(portions)))
    least = 1 if total - largest >= count - 1 else 0
    counts, surplus = [largest] + [least] * (count - 1), total - largest - least * (count - 1)
    while surplus > 0:
        movable = [i for i in range(1, count) if counts[i] < largest] or [i for i in range(1, count) if counts[i] < bound]
        mass, left = sum([portions[i] for i in movable]), surplus
        for i in movable:
            extra = min(bound - counts[i], max(1, left * portions[i] // mass), surplus)
            counts[i] = counts[i] + extra
            surplus = surplus - extra
    return np.array(counts)


def setup_inputs(seed: int = 0) -> dict:
    splits = jax.random.split(jax.random.key(seed), 12)
    dec_hidden = draw_dec_hidden(jax.random.fold_in(splits[11], 71), 0)
    dec_query = draw_dec_query(jax.random.fold_in(splits[11], 71), 0)
    store = draw_store(jax.random.fold_in(splits[11], 71), 0)
    norm_gain = jnp.clip(1.0 + 0.15 * jax.random.normal(splits[3], (E,), jnp.float32), 0.25, 1.75)
    w_query_enc = draw_w_query_enc(jax.random.fold_in(splits[11], 71), 0)
    w_cond = draw_w_cond(jax.random.fold_in(splits[11], 71), 0)
    w_out_enc = draw_w_out_enc(jax.random.fold_in(splits[11], 71), 0)
    w_kv_dec = draw_w_kv_dec(jax.random.fold_in(splits[11], 71), 0)
    owner_keys = jax.random.split(jax.random.fold_in(splits[8], 1), SPANS // CH_DEV)
    owner_turns = jax.random.permutation(jax.random.fold_in(splits[8], 3), SPANS // CH_DEV)
    owner = jax.vmap(lambda own, number: assign_block(jax.random.fold_in(splits[8], 2), own, number, CH_DEV, N_DP, KN, CAP, 2))(owner_keys, owner_turns).reshape((SPANS, KN))
    nb_index = with_ends(jax.random.randint(splits[9], (SPANS, KN), 0, NB_STORE), jax.random.fold_in(splits[9], 1), 0, NB_STORE - 1).astype(jnp.int32)
    nb_count = with_ends(jax.random.randint(splits[10], (SPANS,), 1, KN + 1), jax.random.fold_in(splits[10], 1), 1, KN).astype(jnp.int32)
    return {"dec_hidden": dec_hidden, "dec_query": dec_query, "store": store, "norm_gain": norm_gain, "w_query_enc": w_query_enc, "w_cond": w_cond, "w_out_enc": w_out_enc, "w_kv_dec": w_kv_dec, "owner": owner, "nb_index": nb_index, "nb_count": nb_count}


def reference(dec_hidden, dec_query, store, norm_gain, w_query_enc, w_cond, w_out_enc, w_kv_dec, owner, nb_index, nb_count):
    scale = 1.0 / math.sqrt(HEAD)
    cond = jnp.dot(dec_hidden, w_cond, preferred_element_type=jnp.float32).astype(jnp.bfloat16)
    cond = cond.reshape(SPANS, SPAN, HE, 2 * HEAD)
    store_f = store.astype(jnp.float32)
    normed = (store_f * lax.rsqrt(lax.optimization_barrier(jnp.mean(store_f * store_f, axis=-1, keepdims=True)) + 1e-05) * norm_gain).astype(jnp.bfloat16)
    q_store = jnp.dot(normed.reshape(STORE_ALL * NBLEN, E), w_query_enc, preferred_element_type=jnp.float32).astype(jnp.bfloat16)
    q_store = q_store.reshape(STORE_ALL, NBLEN, HE, HEAD)
    rows_all = (owner * NB_STORE + nb_index).astype(jnp.int32)
    query_all = dec_query.reshape(SPANS, SPAN, HD, HEAD)

    def one_span(items):
        c_cond, c_rows, c_query, c_count = items
        q_pick = jnp.take(q_store, c_rows, axis=0).astype(jnp.float32)
        keys = c_cond[:, :, :HEAD].astype(jnp.float32)
        values = c_cond[:, :, HEAD:].astype(jnp.float32)
        scores = jnp.einsum('nlhd,khd->nhlk', q_pick, keys) * scale
        weights = jax.nn.softmax(scores, axis=-1).astype(jnp.bfloat16).astype(jnp.float32)
        enc_ctx = jnp.einsum('nhlk,khd->nlhd', weights, values).astype(jnp.bfloat16)
        enc_ctx = enc_ctx.reshape(KN * NBLEN, HE * HEAD)
        raw_pick = jnp.take(store, c_rows, axis=0).reshape(KN * NBLEN, E).astype(jnp.float32)
        enc = (raw_pick + jnp.dot(enc_ctx, w_out_enc, preferred_element_type=jnp.float32)).astype(jnp.bfloat16)
        dec_kv = jnp.dot(enc, w_kv_dec, preferred_element_type=jnp.float32).astype(jnp.bfloat16)
        dec_kv = dec_kv.reshape(KN * NBLEN, HD, 2, HEAD).astype(jnp.float32)
        scores2 = jnp.einsum('qhd,jhd->hqj', c_query.astype(jnp.float32), dec_kv[:, :, 0, :]) * scale
        valid = jnp.arange(KN * NBLEN, dtype=jnp.int32) // NBLEN < c_count
        scores2 = jnp.where(valid[None, None, :], scores2, jnp.float32(-1e+30))
        weights2 = jax.nn.softmax(scores2, axis=-1).astype(jnp.bfloat16).astype(jnp.float32)
        out = jnp.einsum('hqj,jhd->qhd', weights2, dec_kv[:, :, 1, :]).astype(jnp.bfloat16)
        return out.reshape(SPAN, HD * HEAD)
    result = lax.map(one_span, (cond, rows_all, query_all, nb_count))
    return result.reshape(TOKENS, HD * HEAD)
```

```python
import functools
import math

import jax
import jax.numpy as jnp
from jax import lax
from jax.experimental import pallas as pl
from jax.experimental.pallas import tpu as pltpu
from jax.sharding import PartitionSpec as P

HEAD = 128
SPAN = 64
NBLEN = 64
KN = 2


def encoder_kernel(scale, slot_ref, q0_ref, q1_ref, own_ref, left_ref, right_ref, ctx_ref):
    cond = (
        own_ref[...].astype(jnp.float32)
        + left_ref[...].astype(jnp.float32)
        + right_ref[...].astype(jnp.float32)
    ).astype(jnp.bfloat16)
    query = jnp.concatenate([q0_ref[0], q1_ref[0]], axis=0)
    for h in range(query.shape[1] // HEAD):
        keys = cond[:, 2 * h * HEAD : (2 * h + 1) * HEAD]
        values = cond[:, (2 * h + 1) * HEAD : (2 * h + 2) * HEAD]
        scores = (
            lax.dot_general(
                query[:, h * HEAD : (h + 1) * HEAD],
                keys,
                (((1,), (1,)), ((), ())),
                preferred_element_type=jnp.float32,
            )
            * scale
        )
        top = jnp.max(scores, axis=-1, keepdims=True)
        weights = jnp.exp(scores - top)
        weights = (weights / jnp.sum(weights, axis=-1, keepdims=True)).astype(jnp.bfloat16)
        ctx_ref[:, h * HEAD : (h + 1) * HEAD] = jnp.dot(
            weights, values, preferred_element_type=jnp.float32
        ).astype(jnp.bfloat16)


def decoder_kernel(
    scale, row_ref, count_ref, s0_ref, s1_ref, c0_ref, c1_ref, c2_ref, c3_ref, w_ref, q_ref, out_ref
):
    ctx = jnp.concatenate([c0_ref[...], c1_ref[...], c2_ref[...], c3_ref[...]], axis=1)
    kv = jnp.dot(ctx, w_ref[...], preferred_element_type=jnp.float32)
    stored = jnp.concatenate([s0_ref[0], s1_ref[0]], axis=0)
    kv = (kv + stored.astype(jnp.float32)).astype(jnp.bfloat16)
    count = count_ref[pl.program_id(0)]
    place = lax.broadcasted_iota(jnp.int32, (SPAN, KN * NBLEN), 1) // NBLEN
    valid = place < count
    for g in range(q_ref.shape[1] // HEAD):
        keys = kv[:, 2 * g * HEAD : (2 * g + 1) * HEAD]
        values = kv[:, (2 * g + 1) * HEAD : (2 * g + 2) * HEAD]
        scores = (
            lax.dot_general(
                q_ref[:, g * HEAD : (g + 1) * HEAD],
                keys,
                (((1,), (1,)), ((), ())),
                preferred_element_type=jnp.float32,
            )
            * scale
        )
        scores = jnp.where(valid, scores, jnp.float32(-1e30))
        top = jnp.max(scores, axis=-1, keepdims=True)
        weights = jnp.exp(scores - top)
        weights = (weights / jnp.sum(weights, axis=-1, keepdims=True)).astype(jnp.bfloat16)
        out_ref[:, g * HEAD : (g + 1) * HEAD] = jnp.dot(
            weights, values, preferred_element_type=jnp.float32
        ).astype(jnp.bfloat16)


def on_device(
    dec_hidden,
    dec_query,
    store,
    norm_gain,
    w_query_enc,
    w_cond,
    w_out_enc,
    w_kv_dec,
    owner,
    nb_index,
    nb_count,
):
    scale = 1.0 / math.sqrt(HEAD)
    n_dp = lax.axis_size("dp")
    n_t = lax.axis_size("tensor")
    rank = lax.axis_index("tensor")
    ahead = [(i, (i + 1) % n_t) for i in range(n_t)]
    back = [(i, (i - 1) % n_t) for i in range(n_t)]
    tokens_here = dec_hidden.shape[0]
    spans = tokens_here // SPAN
    pairs = spans * KN
    capacity = max(2, (pairs + n_dp - 1) // n_dp)
    slots = n_dp * capacity
    width_e = store.shape[2]
    stored = store.shape[0]
    width_q = w_query_enc.shape[1]
    width_kv = w_kv_dec.shape[1]
    width_c = w_cond.shape[1] // n_t
    half_c = width_c // 2
    store_rows = store.reshape(stored * NBLEN, width_e)

    kv_own = jnp.dot(store_rows, w_kv_dec, preferred_element_type=jnp.float32).astype(jnp.bfloat16)
    kv_all = lax.all_gather(kv_own, "dp", axis=0, tiled=True).reshape(-1, NBLEN, width_kv)

    owner_flat = owner.reshape(pairs)
    index_flat = nb_index.reshape(pairs)
    owner_hot = (owner_flat[:, None] == jnp.arange(n_dp, dtype=jnp.int32)[None, :]).astype(jnp.int32)
    before = jnp.cumsum(owner_hot, axis=0) - owner_hot
    place = jnp.sum(before * owner_hot, axis=1)
    slot_of = owner_flat * capacity + place
    wants = jnp.sum(
        jnp.where(
            slot_of[:, None] == jnp.arange(slots, dtype=jnp.int32)[None, :],
            index_flat[:, None],
            0,
        ),
        axis=0,
    ).reshape(n_dp, capacity)
    asked = lax.all_to_all(wants, "dp", split_axis=0, concat_axis=0, tiled=True)
    store_f = store_rows.astype(jnp.float32)
    normed = (
        store_f * lax.rsqrt(jnp.mean(store_f * store_f, axis=-1, keepdims=True) + 1e-05) * norm_gain
    ).astype(jnp.bfloat16)
    q_store = jnp.dot(normed, w_query_enc, preferred_element_type=jnp.float32).astype(jnp.bfloat16)
    pick = (
        asked.reshape(slots)[:, None] == jnp.arange(stored, dtype=jnp.int32)[None, :]
    ).astype(jnp.bfloat16)
    q_send = jnp.einsum(
        "sn,nlf->slf",
        pick,
        q_store.reshape(stored, NBLEN, width_q),
        preferred_element_type=jnp.float32,
    ).astype(jnp.bfloat16)
    q_back = lax.all_to_all(
        q_send.reshape(n_dp, capacity, NBLEN, width_q), "dp", split_axis=0, concat_axis=0, tiled=True
    ).reshape(slots, NBLEN, width_q)

    partial = jnp.dot(dec_hidden, w_cond, preferred_element_type=jnp.float32).astype(jnp.bfloat16)

    def block(which):
        return lax.dynamic_slice_in_dim(partial, lax.rem(which + n_t, n_t) * width_c, width_c, 1)

    far, near_up, near_down, mine = (
        block(rank + 2),
        block(rank + 1),
        block(rank - 1),
        block(rank),
    )
    up_far = lax.ppermute(far[:, :half_c], "tensor", ahead)
    down_far = lax.ppermute(far[:, half_c:], "tensor", back)
    up = jnp.concatenate(
        [
            (near_up[:, :half_c].astype(jnp.float32) + up_far.astype(jnp.float32)).astype(
                jnp.bfloat16
            ),
            near_up[:, half_c:],
        ],
        axis=1,
    )
    down = jnp.concatenate(
        [
            near_down[:, :half_c],
            (near_down[:, half_c:].astype(jnp.float32) + down_far.astype(jnp.float32)).astype(
                jnp.bfloat16
            ),
        ],
        axis=1,
    )
    from_left = lax.ppermute(up, "tensor", ahead)
    from_right = lax.ppermute(down, "tensor", back)

    context = pl.pallas_call(
        functools.partial(encoder_kernel, scale),
        out_shape=jax.ShapeDtypeStruct((pairs * NBLEN, width_q), jnp.bfloat16),
        grid_spec=pltpu.PrefetchScalarGridSpec(
            num_scalar_prefetch=1,
            grid=(spans,),
            in_specs=[
                pl.BlockSpec((1, NBLEN, width_q), lambda c, slot: (slot[2 * c], 0, 0)),
                pl.BlockSpec((1, NBLEN, width_q), lambda c, slot: (slot[2 * c + 1], 0, 0)),
                pl.BlockSpec((SPAN, width_c), lambda c, slot: (c, 0)),
                pl.BlockSpec((SPAN, width_c), lambda c, slot: (c, 0)),
                pl.BlockSpec((SPAN, width_c), lambda c, slot: (c, 0)),
            ],
            out_specs=pl.BlockSpec((KN * NBLEN, width_q), lambda c, slot: (c, 0)),
        ),
        cost_estimate=pl.CostEstimate(
            flops=2 * 2 * pairs * NBLEN * SPAN * width_q,
            bytes_accessed=2 * (2 * pairs * NBLEN * width_q + 3 * tokens_here * width_c),
            transcendentals=pairs * NBLEN * SPAN * 2,
        ),
        name="encoder_attention",
    )(slot_of, q_back, q_back, mine, from_left, from_right)

    w_left = lax.ppermute(w_out_enc, "tensor", ahead)
    w_right = lax.ppermute(w_out_enc, "tensor", back)
    half_w = w_out_enc.shape[1] // 2
    w_far = jnp.concatenate(
        [
            lax.ppermute(w_left[:, :half_w], "tensor", ahead),
            lax.ppermute(w_right[:, half_w:], "tensor", back),
        ],
        axis=1,
    )
    joined = jnp.dot(
        jnp.concatenate([w_out_enc, w_left, w_right, w_far], axis=0),
        w_kv_dec,
        preferred_element_type=jnp.float32,
    ).astype(jnp.bfloat16)

    ctx_left = lax.ppermute(context, "tensor", ahead)
    ctx_right = lax.ppermute(context, "tensor", back)
    half_q = width_q // 2
    ctx_far = jnp.concatenate(
        [
            lax.ppermute(ctx_left[:, :half_q], "tensor", ahead),
            lax.ppermute(ctx_right[:, half_q:], "tensor", back),
        ],
        axis=1,
    )

    rows = owner_flat * stored + index_flat
    heads_width = dec_query.shape[1]
    ctx_spec = pl.BlockSpec((KN * NBLEN, width_q), lambda c, row, count: (c, 0))
    return pl.pallas_call(
        functools.partial(decoder_kernel, scale),
        out_shape=jax.ShapeDtypeStruct((tokens_here, heads_width), jnp.bfloat16),
        grid_spec=pltpu.PrefetchScalarGridSpec(
            num_scalar_prefetch=2,
            grid=(spans,),
            in_specs=[
                pl.BlockSpec((1, NBLEN, width_kv), lambda c, row, count: (row[2 * c], 0, 0)),
                pl.BlockSpec((1, NBLEN, width_kv), lambda c, row, count: (row[2 * c + 1], 0, 0)),
                ctx_spec,
                ctx_spec,
                ctx_spec,
                ctx_spec,
                pl.BlockSpec(joined.shape, lambda c, row, count: (0, 0)),
                pl.BlockSpec((SPAN, heads_width), lambda c, row, count: (c, 0)),
            ],
            out_specs=pl.BlockSpec((SPAN, heads_width), lambda c, row, count: (c, 0)),
        ),
        compiler_params=pltpu.CompilerParams(vmem_limit_bytes=40 << 20),
        cost_estimate=pl.CostEstimate(
            flops=2 * pairs * NBLEN * joined.shape[0] * width_kv,
            bytes_accessed=2 * (pairs * NBLEN * width_kv + joined.size + 2 * dec_query.size),
            transcendentals=tokens_here * KN * NBLEN * heads_width // HEAD,
        ),
        name="decoder_attention",
    )(rows, nb_count, kv_all, kv_all, context, ctx_left, ctx_right, ctx_far, joined, dec_query)


def solution(mesh):
    in_specs = (
        P("dp", "tensor"),
        P("dp", "tensor"),
        P("dp", None, None),
        P(),
        P(None, "tensor"),
        P("tensor", None),
        P("tensor", None),
        P(None, "tensor"),
        P("dp", None),
        P("dp", None),
        P("dp"),
    )
    out_specs = P("dp", "tensor")
    return jax.shard_map(
        on_device, mesh=mesh, in_specs=in_specs, out_specs=out_specs, check_vma=False
    )
```

```python
import functools
import math

import jax
import jax.numpy as jnp
from jax import lax
from jax.experimental import pallas as pl
from jax.experimental.pallas import tpu as pltpu
from jax.sharding import PartitionSpec as P

HEAD = 128
SPAN = 64
NBLEN = 64
KN = 2


def encoder_kernel(scale, slot_ref, q0_ref, q1_ref, own_ref, left_ref, right_ref, ctx_ref):
    cond = (
        own_ref[...].astype(jnp.float32)
        + left_ref[...].astype(jnp.float32)
        + right_ref[...].astype(jnp.float32)
    ).astype(jnp.bfloat16)
    query = jnp.concatenate([q0_ref[0], q1_ref[0]], axis=0)
    for h in range(query.shape[1] // HEAD):
        keys = cond[:, 2 * h * HEAD : (2 * h + 1) * HEAD]
        values = cond[:, (2 * h + 1) * HEAD : (2 * h + 2) * HEAD]
        scores = (
            lax.dot_general(
                query[:, h * HEAD : (h + 1) * HEAD],
                keys,
                (((1,), (1,)), ((), ())),
                preferred_element_type=jnp.float32,
            )
            * scale
        )
        top = jnp.max(scores, axis=-1, keepdims=True)
        weights = jnp.exp(scores - top)
        weights = (weights / jnp.sum(weights, axis=-1, keepdims=True)).astype(jnp.bfloat16)
        ctx_ref[:, h * HEAD : (h + 1) * HEAD] = jnp.dot(
            weights, values, preferred_element_type=jnp.float32
        ).astype(jnp.bfloat16)


def decoder_kernel(scale, pairs, row_ref, count_ref, *refs):
    stored_refs = refs[:pairs]
    c0_ref, c1_ref, c2_ref, c3_ref, w_ref, q_ref, out_ref = refs[pairs:]
    width = c0_ref.shape[1]
    kv = jnp.dot(c0_ref[...], w_ref[:width], preferred_element_type=jnp.float32)
    for i, c_ref in enumerate((c1_ref, c2_ref, c3_ref)):
        kv = kv + jnp.dot(
            c_ref[...], w_ref[(i + 1) * width : (i + 2) * width], preferred_element_type=jnp.float32
        )
    place = lax.broadcasted_iota(jnp.int32, (SPAN, KN * NBLEN), 1) // NBLEN
    spans = pairs // KN
    all_scores = []
    all_values = []
    for c in range(spans):
        stored = jnp.concatenate([stored_refs[KN * c + k][0] for k in range(KN)], axis=0)
        here = (
            kv[c * KN * NBLEN : (c + 1) * KN * NBLEN] + stored.astype(jnp.float32)
        ).astype(jnp.bfloat16)
        all_values.append(here[:, HEAD:])
        scores = (
            lax.dot_general(
                q_ref[c * SPAN : (c + 1) * SPAN],
                here[:, :HEAD],
                (((1,), (1,)), ((), ())),
                preferred_element_type=jnp.float32,
            )
            * scale
        )
        all_scores.append(jnp.where(place < count_ref[c], scores, jnp.float32(-1e30)))
    for c in range(spans):
        scores = all_scores[c]
        weights = jnp.exp(scores - jnp.max(scores, axis=-1, keepdims=True))
        weights = (weights / jnp.sum(weights, axis=-1, keepdims=True)).astype(jnp.bfloat16)
        out_ref[c * SPAN : (c + 1) * SPAN] = jnp.dot(
            weights, all_values[c], preferred_element_type=jnp.float32
        ).astype(jnp.bfloat16)


def on_device(
    dec_hidden,
    dec_query,
    store,
    norm_gain,
    w_query_enc,
    w_cond,
    w_out_enc,
    w_kv_dec,
    owner,
    nb_index,
    nb_count,
):
    scale = 1.0 / math.sqrt(HEAD)
    n_dp = lax.axis_size("dp")
    n_t = lax.axis_size("tensor")
    rank = lax.axis_index("tensor")
    ahead = [(i, (i + 1) % n_t) for i in range(n_t)]
    back = [(i, (i - 1) % n_t) for i in range(n_t)]
    tokens_here = dec_hidden.shape[0]
    spans = tokens_here // SPAN
    pairs = spans * KN
    capacity = max(2, (pairs + n_dp - 1) // n_dp)
    slots = n_dp * capacity
    width_e = store.shape[2]
    stored = store.shape[0]
    width_q = w_query_enc.shape[1]
    width_kv = w_kv_dec.shape[1]
    width_c = w_cond.shape[1] // n_t
    half_c = width_c // 2
    store_rows = store.reshape(stored * NBLEN, width_e)

    kv_own = jnp.dot(store_rows, w_kv_dec, preferred_element_type=jnp.float32).astype(jnp.bfloat16)
    kv_all = lax.all_gather(kv_own, "dp", axis=0, tiled=True).reshape(-1, NBLEN, width_kv)

    owner_flat = owner.reshape(pairs)
    index_flat = nb_index.reshape(pairs)
    owner_hot = (owner_flat[:, None] == jnp.arange(n_dp, dtype=jnp.int32)[None, :]).astype(jnp.int32)
    before = jnp.cumsum(owner_hot, axis=0) - owner_hot
    place = jnp.sum(before * owner_hot, axis=1)
    slot_of = owner_flat * capacity + place
    wants = jnp.sum(
        jnp.where(
            slot_of[:, None] == jnp.arange(slots, dtype=jnp.int32)[None, :],
            index_flat[:, None],
            0,
        ),
        axis=0,
    ).reshape(n_dp, capacity)
    asked = lax.all_to_all(wants, "dp", split_axis=0, concat_axis=0, tiled=True)
    store_f = store_rows.astype(jnp.float32)
    normed = (
        store_f * lax.rsqrt(jnp.mean(store_f * store_f, axis=-1, keepdims=True) + 1e-05) * norm_gain
    ).astype(jnp.bfloat16)
    q_store = jnp.dot(normed, w_query_enc, preferred_element_type=jnp.float32).astype(jnp.bfloat16)
    pick = (
        asked.reshape(slots)[:, None] == jnp.arange(stored, dtype=jnp.int32)[None, :]
    ).astype(jnp.bfloat16)
    q_send = jnp.einsum(
        "sn,nlf->slf",
        pick,
        q_store.reshape(stored, NBLEN, width_q),
        preferred_element_type=jnp.float32,
    ).astype(jnp.bfloat16)
    q_back = lax.all_to_all(
        q_send.reshape(n_dp, capacity, NBLEN, width_q), "dp", split_axis=0, concat_axis=0, tiled=True
    ).reshape(slots, NBLEN, width_q)

    partial = jnp.dot(dec_hidden, w_cond, preferred_element_type=jnp.float32).astype(jnp.bfloat16)

    def block(which):
        return lax.dynamic_slice_in_dim(partial, lax.rem(which + n_t, n_t) * width_c, width_c, 1)

    far, near_up, near_down, mine = (
        block(rank + 2),
        block(rank + 1),
        block(rank - 1),
        block(rank),
    )
    up_far = lax.ppermute(far[:, :half_c], "tensor", ahead)
    down_far = lax.ppermute(far[:, half_c:], "tensor", back)
    up = jnp.concatenate(
        [
            (near_up[:, :half_c].astype(jnp.float32) + up_far.astype(jnp.float32)).astype(
                jnp.bfloat16
            ),
            near_up[:, half_c:],
        ],
        axis=1,
    )
    down = jnp.concatenate(
        [
            near_down[:, :half_c],
            (near_down[:, half_c:].astype(jnp.float32) + down_far.astype(jnp.float32)).astype(
                jnp.bfloat16
            ),
        ],
        axis=1,
    )
    from_left = lax.ppermute(up, "tensor", ahead)
    from_right = lax.ppermute(down, "tensor", back)

    context = pl.pallas_call(
        functools.partial(encoder_kernel, scale),
        out_shape=jax.ShapeDtypeStruct((pairs * NBLEN, width_q), jnp.bfloat16),
        grid_spec=pltpu.PrefetchScalarGridSpec(
            num_scalar_prefetch=1,
            grid=(spans,),
            in_specs=[
                pl.BlockSpec((1, NBLEN, width_q), lambda c, slot: (slot[2 * c], 0, 0)),
                pl.BlockSpec((1, NBLEN, width_q), lambda c, slot: (slot[2 * c + 1], 0, 0)),
                pl.BlockSpec((SPAN, width_c), lambda c, slot: (c, 0)),
                pl.BlockSpec((SPAN, width_c), lambda c, slot: (c, 0)),
                pl.BlockSpec((SPAN, width_c), lambda c, slot: (c, 0)),
            ],
            out_specs=pl.BlockSpec((KN * NBLEN, width_q), lambda c, slot: (c, 0)),
        ),
        cost_estimate=pl.CostEstimate(
            flops=2 * 2 * pairs * NBLEN * SPAN * width_q,
            bytes_accessed=2 * (2 * pairs * NBLEN * width_q + 3 * tokens_here * width_c),
            transcendentals=pairs * NBLEN * SPAN * 2,
        ),
        name="encoder_attention",
    )(slot_of, q_back, q_back, mine, from_left, from_right)

    w_left = lax.ppermute(w_out_enc, "tensor", ahead)
    w_right = lax.ppermute(w_out_enc, "tensor", back)
    half_w = w_out_enc.shape[1] // 2
    w_far = jnp.concatenate(
        [
            lax.ppermute(w_left[:, :half_w], "tensor", ahead),
            lax.ppermute(w_right[:, half_w:], "tensor", back),
        ],
        axis=1,
    )
    joined = jnp.dot(
        jnp.concatenate([w_out_enc, w_left, w_right, w_far], axis=0),
        w_kv_dec,
        preferred_element_type=jnp.float32,
    ).astype(jnp.bfloat16)

    ctx_left = lax.ppermute(context, "tensor", ahead)
    ctx_right = lax.ppermute(context, "tensor", back)
    half_q = width_q // 2
    ctx_far = jnp.concatenate(
        [
            lax.ppermute(ctx_left[:, :half_q], "tensor", ahead),
            lax.ppermute(ctx_right[:, half_q:], "tensor", back),
        ],
        axis=1,
    )

    rows = owner_flat * stored + index_flat
    heads_width = dec_query.shape[1]
    ctx_spec = pl.BlockSpec((pairs * NBLEN, width_q), lambda g, row, count: (0, 0))
    return pl.pallas_call(
        functools.partial(decoder_kernel, scale, pairs),
        out_shape=jax.ShapeDtypeStruct((tokens_here, heads_width), jnp.bfloat16),
        grid_spec=pltpu.PrefetchScalarGridSpec(
            num_scalar_prefetch=2,
            grid=(heads_width // HEAD,),
            in_specs=[
                pl.BlockSpec((1, NBLEN, 2 * HEAD), lambda g, row, count, p=p: (row[p], 0, g))
                for p in range(pairs)
            ]
            + [
                ctx_spec,
                ctx_spec,
                ctx_spec,
                ctx_spec,
                pl.BlockSpec((joined.shape[0], 2 * HEAD), lambda g, row, count: (0, g)),
                pl.BlockSpec((tokens_here, HEAD), lambda g, row, count: (0, g)),
            ],
            out_specs=pl.BlockSpec((tokens_here, HEAD), lambda g, row, count: (0, g)),
        ),
        compiler_params=pltpu.CompilerParams(vmem_limit_bytes=40 << 20),
        cost_estimate=pl.CostEstimate(
            flops=2 * pairs * NBLEN * joined.shape[0] * width_kv,
            bytes_accessed=2 * (pairs * NBLEN * width_kv + joined.size + 2 * dec_query.size),
            transcendentals=tokens_here * KN * NBLEN * heads_width // HEAD,
        ),
        name="decoder_attention",
    )(rows, nb_count, *([kv_all] * pairs), context, ctx_left, ctx_right, ctx_far, joined, dec_query)


def solution(mesh):
    in_specs = (
        P("dp", "tensor"),
        P("dp", "tensor"),
        P("dp", None, None),
        P(),
        P(None, "tensor"),
        P("tensor", None),
        P("tensor", None),
        P(None, "tensor"),
        P("dp", None),
        P("dp", None),
        P("dp"),
    )
    out_specs = P("dp", "tensor")
    return jax.shard_map(
        on_device, mesh=mesh, in_specs=in_specs, out_specs=out_specs, check_vma=False
    )
```

```python
import functools
import math

import jax
import jax.numpy as jnp
from jax import lax
from jax.experimental import pallas as pl
from jax.experimental.pallas import tpu as pltpu
from jax.sharding import PartitionSpec as P

HEAD = 128
SPAN = 64
NBLEN = 64
KN = 2


MESH = pl.DeviceIdType.MESH
SIDE = 4
CORES = 2


class Link:
    def __init__(self, send_sem, recv_sem):
        self.send_sem, self.recv_sem, self.sent = send_sem, recv_sem, []

    def send(self, src, dst, device):
        n = len(self.sent)
        copy = pltpu.make_async_remote_copy(
            src_ref=src,
            dst_ref=dst,
            send_sem=self.send_sem.at[n],
            recv_sem=self.recv_sem.at[n],
            device_id=device,
            device_id_type=MESH,
        )
        copy.start()
        self.sent.append(copy)
        return copy


class Gather:
    def __init__(self, link, own, out):
        self.link, self.own, self.out = link, own, out
        self.y, self.x, self.k, self.t = place()
        self.copies, self.aside = {}, []

    def device(self, half, first, second, core=None):
        x, y = (first, second) if half == 0 else (second, first)
        return dp_index(self.x + x, self.y + y, self.k if core is None else core), self.t

    def at(self, half, first, second, item, count):
        p, s = (self.x, self.y) if half == 0 else (self.y, self.x)
        block = (self.k * SIDE + (s + second) % SIDE) * SIDE + (p + first) % SIDE
        return self.out.at[pl.ds((half * SIDE * SIDE * CORES + block) * 2 + item, count)]

    def source(self, half, block, item, count):
        if self.own is not None and block == (0, 0):
            return self.own.at[pl.ds(half * 2 + item, count)]
        return self.at(half, *block, item, count)

    def to(self, half, name, block, item, count):
        way = {"P+": (1, 0), "P-": (-1, 0), "S+": (0, 1), "S-": (0, -1)}[name[:2]]
        self.copies[half, name] = self.link.send(
            self.source(half, block, item, count),
            self.at(half, *block, item, count),
            self.device(half, *way),
        )

    def side(self, half, block, item, count):
        self.aside.append(
            self.link.send(
                self.source(half, block, item, count),
                self.at(half, *block, item, count),
                self.device(half, 0, 0, 1 - self.k),
            )
        )

    def got(self, half, name, block, item, count):
        self.copies[half, name].wait_recv()
        self.side(half, block, item, count)

    def start(self, h):
        for way in ("P+", "P-", "S+", "S-"):
            self.to(h, way, (0, 0), 0, 2)
        self.side(h, (0, 0), 0, 2)

    def second(self, h):
        self.got(h, "P+", (-1, 0), 0, 2)
        self.to(h, "P+f", (-1, 0), 0, 1)
        self.to(h, "S+l", (-1, 0), 0, 2)
        self.to(h, "S-l", (-1, 0), 0, 2)
        self.got(h, "P-", (1, 0), 0, 2)
        self.to(h, "P-f", (1, 0), 1, 1)
        self.to(h, "S+r", (1, 0), 0, 2)
        self.to(h, "S-r", (1, 0), 0, 2)
        self.got(h, "S+", (0, -1), 0, 2)
        self.to(h, "S+f", (0, -1), 0, 1)
        self.got(h, "S-", (0, 1), 0, 2)
        self.to(h, "S-f", (0, 1), 1, 1)

    def third(self, h):
        self.got(h, "P+f", (-2, 0), 0, 1)
        self.to(h, "S+0", (-2, 0), 0, 1)
        self.to(h, "S-0", (-2, 0), 0, 1)
        self.got(h, "P-f", (2, 0), 1, 1)
        self.to(h, "S+1", (2, 0), 1, 1)
        self.to(h, "S-1", (2, 0), 1, 1)
        self.got(h, "S+l", (-1, -1), 0, 2)
        self.to(h, "S+lf", (-1, -1), 0, 1)
        self.got(h, "S-l", (-1, 1), 0, 2)
        self.to(h, "S-lf", (-1, 1), 1, 1)
        self.got(h, "S+r", (1, -1), 0, 2)
        self.to(h, "S+rf", (1, -1), 0, 1)
        self.got(h, "S-r", (1, 1), 0, 2)
        self.to(h, "S-rf", (1, 1), 1, 1)
        self.got(h, "S+f", (0, -2), 0, 1)
        self.got(h, "S-f", (0, 2), 1, 1)

    def fourth(self, h):
        self.got(h, "S+0", (-2, -1), 0, 1)
        self.to(h, "S+0f", (-2, -1), 0, 1)
        self.got(h, "S-1", (2, 1), 1, 1)
        self.to(h, "S-1f", (2, 1), 1, 1)
        self.got(h, "S+1", (2, -1), 1, 1)
        self.got(h, "S-0", (-2, 1), 0, 1)
        self.got(h, "S+lf", (-1, -2), 0, 1)
        self.got(h, "S-lf", (-1, 2), 1, 1)
        self.got(h, "S+rf", (1, -2), 0, 1)
        self.got(h, "S-rf", (1, 2), 1, 1)

    def fifth(self, h):
        self.got(h, "S+0f", (-2, -2), 0, 1)
        self.got(h, "S-1f", (2, 2), 1, 1)

    def finish(self):
        for copy in self.aside:
            copy.wait_recv()


def dp_index(x, y, core):
    return (y % SIDE * SIDE + x % SIDE) * CORES + core


def place():
    me = lax.axis_index("dp")
    return me // (SIDE * CORES), me // CORES % SIDE, me % CORES, lax.axis_index("tensor")


def item_of(owner, index):
    y, x, core = owner // (SIDE * CORES), owner // CORES % SIDE, owner % CORES
    half = index // 2
    first, second = jnp.where(half == 0, x, y), jnp.where(half == 0, y, x)
    return (((half * CORES + core) * SIDE + second) * SIDE + first) * 2 + index % 2


def exchange_kernel(
    scale,
    n_t,
    items_ref,
    gain_ref,
    store_ref,
    wq_ref,
    wkv_ref,
    hidden_ref,
    wc_ref,
    wout_ref,
    kv_all_ref,
    c_ref,
    store_v,
    wq_v,
    wkv_v,
    hidden_v,
    wc_v,
    wout_v,
    joined_v,
    kv_own_v,
    q_all_v,
    q_sel_v,
    normed_v,
    far_v,
    up_v,
    down_v,
    own_v,
    far_in_v,
    left_v,
    right_v,
    cond_v,
    ctx_v,
    send_sem,
    recv_sem,
    load_sem,
):
    y, x, core, t = place()
    me = lax.axis_index("dp")
    above, below = (me, (t + 1) % n_t), (me, (t + n_t - 1) % n_t)
    twin = (dp_index(x, y, 1 - core), t)
    stored = store_v.shape[0]
    tile = 2 * HEAD
    tiles = wkv_v.shape[1] // tile
    pairs = q_sel_v.shape[0]
    spans = pairs // KN

    loads = [
        pltpu.make_async_copy(src, dst, load_sem.at[n])
        for n, (src, dst) in enumerate(
            (
                (store_ref, store_v),
                (wq_ref, wq_v),
                (wkv_ref, wkv_v),
                (hidden_ref, hidden_v),
                (wc_ref, wc_v),
                (wout_ref, wout_v.at[0]),
            )
        )
    ]
    for load in loads:
        load.start()
    barrier = pltpu.get_barrier_semaphore()
    beside = [
        (dp_index(x + 1, y, core), t),
        (dp_index(x + SIDE - 1, y, core), t),
        (dp_index(x, y + 1, core), t),
        (dp_index(x, y + SIDE - 1, core), t),
        twin,
        above,
        below,
    ]
    for device in beside:
        pl.semaphore_signal(barrier, inc=1, device_id=device, device_id_type=MESH)
    pl.semaphore_wait(barrier, len(beside))

    link = Link(send_sem, recv_sem)
    q_gather = Gather(link, None, q_all_v)
    kv_gather = Gather(link, kv_own_v, kv_all_ref)

    w_up = link.send(wout_ref.at[core], wout_v.at[1, core], above)
    w_down = link.send(wout_ref.at[core], wout_v.at[2, core], below)

    loads[0].wait()
    gain = gain_ref[...]
    for n in range(stored):
        rows = store_v[n].astype(jnp.float32)
        spread = jnp.mean(rows * rows, axis=-1, keepdims=True)
        normed_v[n] = (rows * lax.rsqrt(spread + 1e-05) * gain).astype(jnp.bfloat16)
    loads[1].wait()
    q_own = (
        jnp.dot(
            normed_v[...].reshape(stored * NBLEN, normed_v.shape[2]),
            wq_v[...],
            preferred_element_type=jnp.float32,
        )
        .astype(jnp.bfloat16)
        .reshape(stored, NBLEN, wq_v.shape[1])
    )
    for half in (0, 1):
        q_gather.at(half, 0, 0, 0, 2)[...] = q_own[2 * half : 2 * half + 2]
        q_gather.start(half)

    loads[2].wait()

    def kv_tile(n, carry):
        columns = pl.ds(pl.multiple_of(n * tile, tile), tile)
        kv_own_v[:, :, columns] = (
            jnp.dot(
                store_v[...].reshape(stored * NBLEN, store_v.shape[2]),
                wkv_v[:, columns],
                preferred_element_type=jnp.float32,
            )
            .astype(jnp.bfloat16)
            .reshape(stored, NBLEN, tile)
        )
        return carry

    lax.fori_loop(0, tiles, kv_tile, 0)
    kept = []
    for half in (0, 1):
        copy = pltpu.make_async_copy(
            kv_own_v.at[pl.ds(2 * half, 2)],
            kv_gather.at(half, 0, 0, 0, 2),
            load_sem.at[len(loads) + half],
        )
        copy.start()
        kept.append(copy)
        kv_gather.start(half)

    loads[3].wait()
    loads[4].wait()

    def part(block, half):
        column = ((t + block) % n_t * 2 + half) * tile
        return jnp.dot(
            hidden_v[...],
            wc_v[:, pl.ds(pl.multiple_of(column, tile), tile)],
            preferred_element_type=jnp.float32,
        )

    far_v[0] = part(2, 0).astype(jnp.bfloat16)
    far_up = link.send(far_v.at[0], far_in_v.at[0], above)
    far_v[1] = part(2, 1).astype(jnp.bfloat16)
    far_down = link.send(far_v.at[1], far_in_v.at[1], below)
    for half in (0, 1):
        q_gather.second(half)
    up_v[1] = part(1, 1).astype(jnp.bfloat16)
    near_up = link.send(up_v.at[1], left_v.at[1], above)
    down_v[0] = part(3, 0).astype(jnp.bfloat16)
    near_down = link.send(down_v.at[0], right_v.at[0], below)
    for half in (0, 1):
        q_gather.third(half)
    first_up = part(1, 0)
    first_down = part(3, 1)
    for half in (0, 1):
        q_gather.fourth(half)
    far_up.wait_recv()
    up_v[0] = (first_up + far_in_v[0].astype(jnp.float32)).astype(jnp.bfloat16)
    last_up = link.send(up_v.at[0], left_v.at[0], above)
    far_down.wait_recv()
    down_v[1] = (first_down + far_in_v[1].astype(jnp.float32)).astype(jnp.bfloat16)
    last_down = link.send(down_v.at[1], right_v.at[1], below)

    w_up.wait_recv()
    w_far_up = link.send(wout_v.at[1, core, 0], wout_v.at[3, core, 0], above)
    w_aside = [link.send(wout_v.at[1, core], wout_v.at[1, core], twin)]
    w_down.wait_recv()
    w_far_down = link.send(wout_v.at[2, core, 1], wout_v.at[3, core, 1], below)
    w_aside.append(link.send(wout_v.at[2, core], wout_v.at[2, core], twin))

    own_v[0] = part(0, 0)
    own_v[1] = part(0, 1)
    kv_gather.second(0)
    for half in (0, 1):
        q_gather.fifth(half)

    w_far_up.wait_recv()
    w_aside.append(link.send(wout_v.at[3, core, 0], wout_v.at[3, core, 0], twin))
    w_far_down.wait_recv()
    w_aside.append(link.send(wout_v.at[3, core, 1], wout_v.at[3, core, 1], twin))
    q_gather.finish()

    def pick(p, carry):
        q_sel_v[p] = q_all_v[items_ref[p]]
        return carry

    lax.fori_loop(0, pairs, pick, 0)
    loads[5].wait()
    for copy in w_aside:
        copy.wait_recv()

    def joined_tile(n, carry):
        columns = pl.ds(pl.multiple_of(n * tile, tile), tile)
        joined_v[:, columns] = jnp.dot(
            wout_v[...].reshape(joined_v.shape[0], wout_v.shape[4]),
            wkv_v[:, columns],
            preferred_element_type=jnp.float32,
        ).astype(jnp.bfloat16)
        return carry

    lax.fori_loop(0, tiles, joined_tile, 0)
    kv_gather.second(1)

    for copy in (near_up, near_down, last_up, last_down):
        copy.wait_recv()
    for h in range(2):
        cond_v[h] = (
            own_v[h] + left_v[h].astype(jnp.float32) + right_v[h].astype(jnp.float32)
        ).astype(jnp.bfloat16)
    for h in range(2):
        query = q_sel_v[:, :, h * HEAD : (h + 1) * HEAD].reshape(spans, KN * NBLEN, HEAD)
        keys = cond_v[h, :, :HEAD].reshape(spans, SPAN, HEAD)
        values = cond_v[h, :, HEAD:].reshape(spans, SPAN, HEAD)
        scores = (
            jnp.einsum("cld,ckd->clk", query, keys, preferred_element_type=jnp.float32) * scale
        )
        weights = jnp.exp(scores - jnp.max(scores, axis=-1, keepdims=True))
        weights = (weights / jnp.sum(weights, axis=-1, keepdims=True)).astype(jnp.bfloat16)
        context = jnp.einsum("clk,ckd->cld", weights, values, preferred_element_type=jnp.float32)
        ctx_v[0, :, :, h * HEAD : (h + 1) * HEAD] = context.astype(jnp.bfloat16).reshape(
            ctx_v.shape[1], ctx_v.shape[2], HEAD
        )
    ctx_up = link.send(ctx_v.at[0], ctx_v.at[1], above)
    ctx_down = link.send(ctx_v.at[0], ctx_v.at[2], below)
    ctx_up.wait_recv()
    ctx_far_up = link.send(ctx_v.at[1, 0], ctx_v.at[3, 0], above)
    ctx_down.wait_recv()
    ctx_far_down = link.send(ctx_v.at[2, 1], ctx_v.at[3, 1], below)

    for half in (0, 1):
        kv_gather.third(half)
    ctx_far_up.wait_recv()
    ctx_far_down.wait_recv()
    rows = ctx_v.shape[1] * ctx_v.shape[2]

    def c_tile(n, carry):
        columns = pl.ds(pl.multiple_of(n * tile, tile), tile)
        total = None
        for j in range(ctx_v.shape[0]):
            term = jnp.dot(
                ctx_v[j].reshape(rows, ctx_v.shape[3]),
                joined_v[j * ctx_v.shape[3] : (j + 1) * ctx_v.shape[3], columns],
                preferred_element_type=jnp.float32,
            )
            total = term if total is None else total + term
        wc_v[:rows, columns] = total.astype(jnp.bfloat16)
        return carry

    lax.fori_loop(0, tiles, c_tile, 0)
    out = pltpu.make_async_copy(wc_v.at[pl.ds(0, rows)], c_ref, load_sem.at[len(loads) + 2])
    out.start()
    for half in (0, 1):
        kv_gather.fourth(half)
    for half in (0, 1):
        kv_gather.fifth(half)
    kv_gather.finish()
    out.wait()
    for copy in kept:
        copy.wait()
    for copy in link.sent:
        copy.wait_send()


def decoder_kernel(scale, pairs, row_ref, count_ref, *refs):
    stored_refs = refs[:pairs]
    c_ref, q_ref, out_ref = refs[pairs:]
    key_place = lax.broadcasted_iota(jnp.int32, (SPAN, KN * NBLEN), 1) // NBLEN
    spans = pairs // KN
    all_scores = []
    all_values = []
    for c in range(spans):
        stored = jnp.concatenate([stored_refs[KN * c + k][0] for k in range(KN)], axis=0)
        here = (
            c_ref[c * KN * NBLEN : (c + 1) * KN * NBLEN].astype(jnp.float32)
            + stored.astype(jnp.float32)
        ).astype(jnp.bfloat16)
        all_values.append(here[:, HEAD:])
        scores = (
            lax.dot_general(
                q_ref[c * SPAN : (c + 1) * SPAN],
                here[:, :HEAD],
                (((1,), (1,)), ((), ())),
                preferred_element_type=jnp.float32,
            )
            * scale
        )
        all_scores.append(jnp.where(key_place < count_ref[c], scores, jnp.float32(-1e30)))
    for c in range(spans):
        scores = all_scores[c]
        weights = jnp.exp(scores - jnp.max(scores, axis=-1, keepdims=True))
        weights = (weights / jnp.sum(weights, axis=-1, keepdims=True)).astype(jnp.bfloat16)
        out_ref[c * SPAN : (c + 1) * SPAN] = jnp.dot(
            weights, all_values[c], preferred_element_type=jnp.float32
        ).astype(jnp.bfloat16)


def on_device(
    dec_hidden,
    dec_query,
    store,
    norm_gain,
    w_query_enc,
    w_cond,
    w_out_enc,
    w_kv_dec,
    owner,
    nb_index,
    nb_count,
):
    scale = 1.0 / math.sqrt(HEAD)
    n_t = lax.axis_size("tensor")
    tokens = dec_hidden.shape[0]
    spans = tokens // SPAN
    pairs = spans * KN
    rows = pairs * NBLEN
    stored, _, width_e = store.shape
    width_q = w_query_enc.shape[1]
    width_kv = w_kv_dec.shape[1]
    items = item_of(owner, nb_index).reshape(pairs)
    bf16, f32 = jnp.bfloat16, jnp.float32
    quarter = w_out_enc.shape[0] // 4
    half_c = 2 * HEAD
    anywhere = pl.BlockSpec(memory_space=pl.ANY)
    copies = 2 * 90 + 8 + 6 + 4
    kv_all, extra = pl.pallas_call(
        functools.partial(exchange_kernel, scale, n_t),
        out_shape=(
            jax.ShapeDtypeStruct((lax.axis_size("dp") * stored, NBLEN, width_kv), bf16),
            jax.ShapeDtypeStruct((rows, width_kv), bf16),
        ),
        in_specs=[
            pl.BlockSpec(memory_space=pltpu.SMEM),
            pl.BlockSpec(memory_space=pltpu.VMEM),
        ]
        + [anywhere] * 6,
        out_specs=(anywhere, anywhere),
        scratch_shapes=[
            pltpu.VMEM((stored, NBLEN, width_e), bf16),
            pltpu.VMEM(w_query_enc.shape, bf16),
            pltpu.VMEM(w_kv_dec.shape, bf16),
            pltpu.VMEM(dec_hidden.shape, bf16),
            pltpu.VMEM(w_cond.shape, bf16),
            pltpu.VMEM((n_t, 2, 2, quarter, width_e), bf16),
            pltpu.VMEM((n_t * w_out_enc.shape[0], width_kv), bf16),
            pltpu.VMEM((stored, NBLEN, width_kv), bf16),
            pltpu.VMEM((lax.axis_size("dp") * stored, NBLEN, width_q), bf16),
            pltpu.VMEM((pairs, NBLEN, width_q), bf16),
            pltpu.VMEM((stored, NBLEN, width_e), bf16),
            pltpu.VMEM((2, tokens, half_c), bf16),
            pltpu.VMEM((2, tokens, half_c), bf16),
            pltpu.VMEM((2, tokens, half_c), bf16),
            pltpu.VMEM((2, tokens, half_c), f32),
            pltpu.VMEM((2, tokens, half_c), bf16),
            pltpu.VMEM((2, tokens, half_c), bf16),
            pltpu.VMEM((2, tokens, half_c), bf16),
            pltpu.VMEM((2, tokens, half_c), bf16),
            pltpu.VMEM((n_t, 2, rows // 2, width_q), bf16),
            pltpu.SemaphoreType.DMA((copies,)),
            pltpu.SemaphoreType.DMA((copies,)),
            pltpu.SemaphoreType.DMA((9,)),
        ],
        compiler_params=pltpu.CompilerParams(
            collective_id=0, has_side_effects=True, vmem_limit_bytes=60 << 20
        ),
        name="exchange",
    )(
        items,
        norm_gain.reshape(1, width_e),
        store,
        w_query_enc,
        w_kv_dec,
        dec_hidden,
        w_cond,
        w_out_enc.reshape(2, 2, quarter, width_e),
    )

    heads_width = dec_query.shape[1]
    return pl.pallas_call(
        functools.partial(decoder_kernel, scale, pairs),
        out_shape=jax.ShapeDtypeStruct((tokens, heads_width), bf16),
        grid_spec=pltpu.PrefetchScalarGridSpec(
            num_scalar_prefetch=2,
            grid=(heads_width // HEAD,),
            in_specs=[
                pl.BlockSpec((1, NBLEN, 2 * HEAD), lambda g, row, count, p=p: (row[p], 0, g))
                for p in range(pairs)
            ]
            + [
                pl.BlockSpec((rows, 2 * HEAD), lambda g, row, count: (0, g)),
                pl.BlockSpec((tokens, HEAD), lambda g, row, count: (0, g)),
            ],
            out_specs=pl.BlockSpec((tokens, HEAD), lambda g, row, count: (0, g)),
        ),
        compiler_params=pltpu.CompilerParams(vmem_limit_bytes=40 << 20),
        name="decoder_attention",
    )(items, nb_count, *([kv_all] * pairs), extra, dec_query)


def solution(mesh):
    in_specs = (
        P("dp", "tensor"),
        P("dp", "tensor"),
        P("dp", None, None),
        P(),
        P(None, "tensor"),
        P("tensor", None),
        P("tensor", None),
        P(None, "tensor"),
        P("dp", None),
        P("dp", None),
        P("dp"),
    )
    out_specs = P("dp", "tensor")
    return jax.shard_map(
        on_device, mesh=mesh, in_specs=in_specs, out_specs=out_specs, check_vma=False
    )
```

```python
import functools
import math

import jax
import jax.numpy as jnp
from jax import lax
from jax.experimental import pallas as pl
from jax.experimental.pallas import tpu as pltpu
from jax.sharding import PartitionSpec as P

HEAD = 128
SPAN = 64
NBLEN = 64
KN = 2


MESH = pl.DeviceIdType.MESH
SIDE = 4
CORES = 2


class Link:
    def __init__(self, send_sem, recv_sem):
        self.send_sem, self.recv_sem, self.sent = send_sem, recv_sem, []

    def send(self, src, dst, device):
        n = len(self.sent)
        copy = pltpu.make_async_remote_copy(
            src_ref=src,
            dst_ref=dst,
            send_sem=self.send_sem.at[n],
            recv_sem=self.recv_sem.at[n],
            device_id=device,
            device_id_type=MESH,
        )
        copy.start()
        self.sent.append(copy)
        return copy


class Gather:
    def __init__(self, link, own, out):
        self.link, self.own, self.out = link, own, out
        self.y, self.x, self.k, self.t = place()
        self.copies, self.aside, self.first = {}, [], {}

    def device(self, half, first, second, core=None):
        x, y = (first, second) if half == 0 else (second, first)
        return dp_index(self.x + x, self.y + y, self.k if core is None else core), self.t

    def at(self, half, first, second, item, count):
        p, s = (self.x, self.y) if half == 0 else (self.y, self.x)
        block = (self.k * SIDE + (s + second) % SIDE) * SIDE + (p + first) % SIDE
        return self.out.at[pl.ds((half * SIDE * SIDE * CORES + block) * 2 + item, count)]

    def source(self, half, block, item, count):
        if self.own is not None and block == (0, 0):
            return self.own.at[pl.ds(half * 2 + item, count)]
        return self.at(half, *block, item, count)

    def to(self, half, name, block, item, count):
        way = {"P+": (1, 0), "P-": (-1, 0), "S+": (0, 1), "S-": (0, -1)}[name[:2]]
        self.copies[half, name] = self.link.send(
            self.source(half, block, item, count),
            self.at(half, *block, item, count),
            self.device(half, *way),
        )

    def side(self, half, block, item, count):
        self.aside.append(
            self.link.send(
                self.source(half, block, item, count),
                self.at(half, *block, item, count),
                self.device(half, 0, 0, 1 - self.k),
            )
        )

    def got(self, half, name, block, item, count):
        self.copies[half, name].wait_recv()
        self.side(half, block, item, count)

    def start(self, h, item, count):
        for way in ("P+", "P-", "S+", "S-"):
            self.to(h, f"{way} {item}", (0, 0), item, count)
        self.side(h, (0, 0), item, count)
        self.first.setdefault(h, []).append((item, count))

    def arrived(self, h, way, block):
        for item, count in self.first[h]:
            self.got(h, f"{way} {item}", block, item, count)

    def second(self, h):
        self.arrived(h, "P+", (-1, 0))
        self.to(h, "P+f", (-1, 0), 0, 1)
        self.to(h, "S+l", (-1, 0), 0, 2)
        self.to(h, "S-l", (-1, 0), 0, 2)
        self.arrived(h, "P-", (1, 0))
        self.to(h, "P-f", (1, 0), 1, 1)
        self.to(h, "S+r", (1, 0), 0, 2)
        self.to(h, "S-r", (1, 0), 0, 2)
        self.arrived(h, "S+", (0, -1))
        self.to(h, "S+f", (0, -1), 0, 1)
        self.arrived(h, "S-", (0, 1))
        self.to(h, "S-f", (0, 1), 1, 1)

    def third(self, h):
        self.got(h, "P+f", (-2, 0), 0, 1)
        self.to(h, "S+0", (-2, 0), 0, 1)
        self.to(h, "S-0", (-2, 0), 0, 1)
        self.got(h, "P-f", (2, 0), 1, 1)
        self.to(h, "S+1", (2, 0), 1, 1)
        self.to(h, "S-1", (2, 0), 1, 1)
        self.got(h, "S+l", (-1, -1), 0, 2)
        self.to(h, "S+lf", (-1, -1), 0, 1)
        self.got(h, "S-l", (-1, 1), 0, 2)
        self.to(h, "S-lf", (-1, 1), 1, 1)
        self.got(h, "S+r", (1, -1), 0, 2)
        self.to(h, "S+rf", (1, -1), 0, 1)
        self.got(h, "S-r", (1, 1), 0, 2)
        self.to(h, "S-rf", (1, 1), 1, 1)
        self.got(h, "S+f", (0, -2), 0, 1)
        self.got(h, "S-f", (0, 2), 1, 1)

    def fourth(self, h):
        self.got(h, "S+0", (-2, -1), 0, 1)
        self.to(h, "S+0f", (-2, -1), 0, 1)
        self.got(h, "S-1", (2, 1), 1, 1)
        self.to(h, "S-1f", (2, 1), 1, 1)
        self.got(h, "S+1", (2, -1), 1, 1)
        self.got(h, "S-0", (-2, 1), 0, 1)
        self.got(h, "S+lf", (-1, -2), 0, 1)
        self.got(h, "S-lf", (-1, 2), 1, 1)
        self.got(h, "S+rf", (1, -2), 0, 1)
        self.got(h, "S-rf", (1, 2), 1, 1)

    def fifth(self, h):
        self.got(h, "S+0f", (-2, -2), 0, 1)
        self.got(h, "S-1f", (2, 2), 1, 1)

    def finish(self):
        for copy in self.aside:
            copy.wait_recv()


def dp_index(x, y, core):
    return (y % SIDE * SIDE + x % SIDE) * CORES + core


def place():
    me = lax.axis_index("dp")
    return me // (SIDE * CORES), me // CORES % SIDE, me % CORES, lax.axis_index("tensor")


def item_of(owner, index):
    y, x, core = owner // (SIDE * CORES), owner // CORES % SIDE, owner % CORES
    half = index // 2
    first, second = jnp.where(half == 0, x, y), jnp.where(half == 0, y, x)
    return (((half * CORES + core) * SIDE + second) * SIDE + first) * 2 + index % 2


def exchange_kernel(
    scale,
    n_t,
    items_ref,
    gain_ref,
    store_ref,
    wq_ref,
    wkv_ref,
    hidden_ref,
    wc_ref,
    wout_ref,
    kv_all_ref,
    c_ref,
    store_v,
    wq_v,
    wkv_v,
    hidden_v,
    wc_v,
    wout_v,
    joined_v,
    kv_own_v,
    q_all_v,
    q_sel_v,
    normed_v,
    far_v,
    up_v,
    down_v,
    own_v,
    far_in_v,
    left_v,
    right_v,
    cond_v,
    ctx_v,
    send_sem,
    recv_sem,
    load_sem,
):
    y, x, core, t = place()
    me = lax.axis_index("dp")
    above, below = (me, (t + 1) % n_t), (me, (t + n_t - 1) % n_t)
    twin = (dp_index(x, y, 1 - core), t)
    stored = store_v.shape[0]
    tile = 2 * HEAD
    tiles = wkv_v.shape[1] // tile
    pairs = q_sel_v.shape[0]
    spans = pairs // KN

    loads = [
        pltpu.make_async_copy(src, dst, load_sem.at[n])
        for n, (src, dst) in enumerate(
            (
                (store_ref, store_v),
                (wq_ref, wq_v),
                (wkv_ref, wkv_v),
                (hidden_ref, hidden_v),
                (wc_ref, wc_v),
                (wout_ref, wout_v.at[0]),
            )
        )
    ]
    for load in loads[:3]:
        load.start()
    barrier = pltpu.get_barrier_semaphore()
    beside = [
        (dp_index(x + 1, y, core), t),
        (dp_index(x + SIDE - 1, y, core), t),
        (dp_index(x, y + 1, core), t),
        (dp_index(x, y + SIDE - 1, core), t),
        twin,
        above,
        below,
    ]
    for device in beside:
        pl.semaphore_signal(barrier, inc=1, device_id=device, device_id_type=MESH)
    pl.semaphore_wait(barrier, len(beside))

    link = Link(send_sem, recv_sem)
    q_gather = Gather(link, None, q_all_v)
    kv_gather = Gather(link, kv_own_v, kv_all_ref)

    w_up = link.send(wout_ref.at[core], wout_v.at[1, core], above)
    w_down = link.send(wout_ref.at[core], wout_v.at[2, core], below)

    loads[0].wait()
    gain = gain_ref[...]
    for n in range(stored):
        rows = store_v[n].astype(jnp.float32)
        spread = jnp.mean(rows * rows, axis=-1, keepdims=True)
        normed_v[n] = (rows * lax.rsqrt(spread + 1e-05) * gain).astype(jnp.bfloat16)
    loads[1].wait()
    q_own = (
        jnp.dot(
            normed_v[...].reshape(stored * NBLEN, normed_v.shape[2]),
            wq_v[...],
            preferred_element_type=jnp.float32,
        )
        .astype(jnp.bfloat16)
        .reshape(stored, NBLEN, wq_v.shape[1])
    )
    for half in (0, 1):
        q_gather.at(half, 0, 0, 0, 2)[...] = q_own[2 * half : 2 * half + 2]
        q_gather.start(half, 0, 2)

    loads[2].wait()
    for load in loads[3:]:
        load.start()

    def kv_tile(n, carry):
        columns = pl.ds(pl.multiple_of(n * tile, tile), tile)
        kv_own_v[:, :, columns] = (
            jnp.dot(
                store_v[...].reshape(stored * NBLEN, store_v.shape[2]),
                wkv_v[:, columns],
                preferred_element_type=jnp.float32,
            )
            .astype(jnp.bfloat16)
            .reshape(stored, NBLEN, tile)
        )
        return carry

    lax.fori_loop(0, tiles, kv_tile, 0)
    kv_gather.start(0, 0, 1)
    for half in (0, 1):
        q_gather.second(half)
    kept = []
    for half in (0, 1):
        copy = pltpu.make_async_copy(
            kv_own_v.at[pl.ds(2 * half, 2)],
            kv_gather.at(half, 0, 0, 0, 2),
            load_sem.at[len(loads) + half],
        )
        copy.start()
        kept.append(copy)

    loads[3].wait()
    loads[4].wait()

    def part(block, half):
        column = ((t + block) % n_t * 2 + half) * tile
        return jnp.dot(
            hidden_v[...],
            wc_v[:, pl.ds(pl.multiple_of(column, tile), tile)],
            preferred_element_type=jnp.float32,
        )

    far_v[0] = part(2, 0).astype(jnp.bfloat16)
    far_up = link.send(far_v.at[0], far_in_v.at[0], above)
    far_v[1] = part(2, 1).astype(jnp.bfloat16)
    far_down = link.send(far_v.at[1], far_in_v.at[1], below)
    kv_gather.start(0, 1, 1)
    for half in (0, 1):
        q_gather.third(half)
    kv_gather.start(1, 0, 1)
    up_v[1] = part(1, 1).astype(jnp.bfloat16)
    near_up = link.send(up_v.at[1], left_v.at[1], above)
    down_v[0] = part(3, 0).astype(jnp.bfloat16)
    near_down = link.send(down_v.at[0], right_v.at[0], below)
    for half in (0, 1):
        q_gather.fourth(half)
    kv_gather.start(1, 1, 1)
    first_up = part(1, 0)
    first_down = part(3, 1)
    far_up.wait_recv()
    up_v[0] = (first_up + far_in_v[0].astype(jnp.float32)).astype(jnp.bfloat16)
    last_up = link.send(up_v.at[0], left_v.at[0], above)
    far_down.wait_recv()
    down_v[1] = (first_down + far_in_v[1].astype(jnp.float32)).astype(jnp.bfloat16)
    last_down = link.send(down_v.at[1], right_v.at[1], below)

    w_up.wait_recv()
    w_far_up = link.send(wout_v.at[1, core, 0], wout_v.at[3, core, 0], above)
    w_aside = [link.send(wout_v.at[1, core], wout_v.at[1, core], twin)]
    w_down.wait_recv()
    w_far_down = link.send(wout_v.at[2, core, 1], wout_v.at[3, core, 1], below)
    w_aside.append(link.send(wout_v.at[2, core], wout_v.at[2, core], twin))
    kv_gather.second(0)
    own_v[0] = part(0, 0)
    own_v[1] = part(0, 1)
    for half in (0, 1):
        q_gather.fifth(half)
    q_gather.finish()

    def pick(p, carry):
        q_sel_v[p] = q_all_v[items_ref[p]]
        return carry

    lax.fori_loop(0, pairs, pick, 0)
    kv_gather.second(1)

    for copy in (near_up, near_down, last_up, last_down):
        copy.wait_recv()
    for h in range(2):
        cond_v[h] = (
            own_v[h] + left_v[h].astype(jnp.float32) + right_v[h].astype(jnp.float32)
        ).astype(jnp.bfloat16)
    for h in range(2):
        query = q_sel_v[:, :, h * HEAD : (h + 1) * HEAD].reshape(spans, KN * NBLEN, HEAD)
        keys = cond_v[h, :, :HEAD].reshape(spans, SPAN, HEAD)
        values = cond_v[h, :, HEAD:].reshape(spans, SPAN, HEAD)
        scores = (
            jnp.einsum("cld,ckd->clk", query, keys, preferred_element_type=jnp.float32) * scale
        )
        weights = jnp.exp(scores - jnp.max(scores, axis=-1, keepdims=True))
        weights = (weights / jnp.sum(weights, axis=-1, keepdims=True)).astype(jnp.bfloat16)
        context = jnp.einsum("clk,ckd->cld", weights, values, preferred_element_type=jnp.float32)
        ctx_v[0, :, :, h * HEAD : (h + 1) * HEAD] = context.astype(jnp.bfloat16).reshape(
            ctx_v.shape[1], ctx_v.shape[2], HEAD
        )
    ctx_up = link.send(ctx_v.at[0], ctx_v.at[1], above)
    ctx_down = link.send(ctx_v.at[0], ctx_v.at[2], below)

    w_far_up.wait_recv()
    w_aside.append(link.send(wout_v.at[3, core, 0], wout_v.at[3, core, 0], twin))
    w_far_down.wait_recv()
    w_aside.append(link.send(wout_v.at[3, core, 1], wout_v.at[3, core, 1], twin))
    loads[5].wait()
    for copy in w_aside:
        copy.wait_recv()

    def joined_tile(n, carry):
        columns = pl.ds(pl.multiple_of(n * tile, tile), tile)
        joined_v[:, columns] = jnp.dot(
            wout_v[...].reshape(joined_v.shape[0], wout_v.shape[4]),
            wkv_v[:, columns],
            preferred_element_type=jnp.float32,
        ).astype(jnp.bfloat16)
        return carry

    lax.fori_loop(0, tiles, joined_tile, 0)

    ctx_up.wait_recv()
    ctx_far_up = link.send(ctx_v.at[1, 0], ctx_v.at[3, 0], above)
    ctx_down.wait_recv()
    ctx_far_down = link.send(ctx_v.at[2, 1], ctx_v.at[3, 1], below)

    for half in (0, 1):
        kv_gather.third(half)
    ctx_far_up.wait_recv()
    ctx_far_down.wait_recv()
    rows = ctx_v.shape[1] * ctx_v.shape[2]

    def c_tile(n, carry):
        columns = pl.ds(pl.multiple_of(n * tile, tile), tile)
        total = None
        for j in range(ctx_v.shape[0]):
            term = jnp.dot(
                ctx_v[j].reshape(rows, ctx_v.shape[3]),
                joined_v[j * ctx_v.shape[3] : (j + 1) * ctx_v.shape[3], columns],
                preferred_element_type=jnp.float32,
            )
            total = term if total is None else total + term
        wc_v[:rows, columns] = total.astype(jnp.bfloat16)
        return carry

    lax.fori_loop(0, tiles, c_tile, 0)
    out = pltpu.make_async_copy(wc_v.at[pl.ds(0, rows)], c_ref, load_sem.at[len(loads) + 2])
    out.start()
    for half in (0, 1):
        kv_gather.fourth(half)
    for half in (0, 1):
        kv_gather.fifth(half)
    kv_gather.finish()
    out.wait()
    for copy in kept:
        copy.wait()
    for copy in link.sent:
        copy.wait_send()


def decoder_kernel(scale, pairs, row_ref, count_ref, *refs):
    stored_refs = refs[:pairs]
    c_ref, q_ref, out_ref = refs[pairs:]
    key_place = lax.broadcasted_iota(jnp.int32, (SPAN, KN * NBLEN), 1) // NBLEN
    spans = pairs // KN
    all_scores = []
    all_values = []
    for c in range(spans):
        stored = jnp.concatenate([stored_refs[KN * c + k][0] for k in range(KN)], axis=0)
        here = (
            c_ref[c * KN * NBLEN : (c + 1) * KN * NBLEN].astype(jnp.float32)
            + stored.astype(jnp.float32)
        ).astype(jnp.bfloat16)
        all_values.append(here[:, HEAD:])
        scores = (
            lax.dot_general(
                q_ref[c * SPAN : (c + 1) * SPAN],
                here[:, :HEAD],
                (((1,), (1,)), ((), ())),
                preferred_element_type=jnp.float32,
            )
            * scale
        )
        all_scores.append(jnp.where(key_place < count_ref[c], scores, jnp.float32(-1e30)))
    for c in range(spans):
        scores = all_scores[c]
        weights = jnp.exp(scores - jnp.max(scores, axis=-1, keepdims=True))
        weights = (weights / jnp.sum(weights, axis=-1, keepdims=True)).astype(jnp.bfloat16)
        out_ref[c * SPAN : (c + 1) * SPAN] = jnp.dot(
            weights, all_values[c], preferred_element_type=jnp.float32
        ).astype(jnp.bfloat16)


def on_device(
    dec_hidden,
    dec_query,
    store,
    norm_gain,
    w_query_enc,
    w_cond,
    w_out_enc,
    w_kv_dec,
    owner,
    nb_index,
    nb_count,
):
    scale = 1.0 / math.sqrt(HEAD)
    n_t = lax.axis_size("tensor")
    tokens = dec_hidden.shape[0]
    spans = tokens // SPAN
    pairs = spans * KN
    rows = pairs * NBLEN
    stored, _, width_e = store.shape
    width_q = w_query_enc.shape[1]
    width_kv = w_kv_dec.shape[1]
    items = item_of(owner, nb_index).reshape(pairs)
    bf16, f32 = jnp.bfloat16, jnp.float32
    quarter = w_out_enc.shape[0] // 4
    half_c = 2 * HEAD
    anywhere = pl.BlockSpec(memory_space=pl.ANY)
    copies = 2 * 90 + 20 + 8 + 6 + 4
    kv_all, extra = pl.pallas_call(
        functools.partial(exchange_kernel, scale, n_t),
        out_shape=(
            jax.ShapeDtypeStruct((lax.axis_size("dp") * stored, NBLEN, width_kv), bf16),
            jax.ShapeDtypeStruct((rows, width_kv), bf16),
        ),
        in_specs=[
            pl.BlockSpec(memory_space=pltpu.SMEM),
            pl.BlockSpec(memory_space=pltpu.VMEM),
        ]
        + [anywhere] * 6,
        out_specs=(anywhere, anywhere),
        scratch_shapes=[
            pltpu.VMEM((stored, NBLEN, width_e), bf16),
            pltpu.VMEM(w_query_enc.shape, bf16),
            pltpu.VMEM(w_kv_dec.shape, bf16),
            pltpu.VMEM(dec_hidden.shape, bf16),
            pltpu.VMEM(w_cond.shape, bf16),
            pltpu.VMEM((n_t, 2, 2, quarter, width_e), bf16),
            pltpu.VMEM((n_t * w_out_enc.shape[0], width_kv), bf16),
            pltpu.VMEM((stored, NBLEN, width_kv), bf16),
            pltpu.VMEM((lax.axis_size("dp") * stored, NBLEN, width_q), bf16),
            pltpu.VMEM((pairs, NBLEN, width_q), bf16),
            pltpu.VMEM((stored, NBLEN, width_e), bf16),
            pltpu.VMEM((2, tokens, half_c), bf16),
            pltpu.VMEM((2, tokens, half_c), bf16),
            pltpu.VMEM((2, tokens, half_c), bf16),
            pltpu.VMEM((2, tokens, half_c), f32),
            pltpu.VMEM((2, tokens, half_c), bf16),
            pltpu.VMEM((2, tokens, half_c), bf16),
            pltpu.VMEM((2, tokens, half_c), bf16),
            pltpu.VMEM((2, tokens, half_c), bf16),
            pltpu.VMEM((n_t, 2, rows // 2, width_q), bf16),
            pltpu.SemaphoreType.DMA((copies,)),
            pltpu.SemaphoreType.DMA((copies,)),
            pltpu.SemaphoreType.DMA((9,)),
        ],
        compiler_params=pltpu.CompilerParams(
            collective_id=0, has_side_effects=True, vmem_limit_bytes=60 << 20
        ),
        name="exchange",
    )(
        items,
        norm_gain.reshape(1, width_e),
        store,
        w_query_enc,
        w_kv_dec,
        dec_hidden,
        w_cond,
        w_out_enc.reshape(2, 2, quarter, width_e),
    )

    heads_width = dec_query.shape[1]
    return pl.pallas_call(
        functools.partial(decoder_kernel, scale, pairs),
        out_shape=jax.ShapeDtypeStruct((tokens, heads_width), bf16),
        grid_spec=pltpu.PrefetchScalarGridSpec(
            num_scalar_prefetch=2,
            grid=(heads_width // HEAD,),
            in_specs=[
                pl.BlockSpec((1, NBLEN, 2 * HEAD), lambda g, row, count, p=p: (row[p], 0, g))
                for p in range(pairs)
            ]
            + [
                pl.BlockSpec((rows, 2 * HEAD), lambda g, row, count: (0, g)),
                pl.BlockSpec((tokens, HEAD), lambda g, row, count: (0, g)),
            ],
            out_specs=pl.BlockSpec((tokens, HEAD), lambda g, row, count: (0, g)),
        ),
        compiler_params=pltpu.CompilerParams(vmem_limit_bytes=56 << 20),
        name="decoder_attention",
    )(items, nb_count, *([kv_all] * pairs), extra, dec_query)


def solution(mesh):
    in_specs = (
        P("dp", "tensor"),
        P("dp", "tensor"),
        P("dp", None, None),
        P(),
        P(None, "tensor"),
        P("tensor", None),
        P("tensor", None),
        P(None, "tensor"),
        P("dp", None),
        P("dp", None),
        P("dp"),
    )
    out_specs = P("dp", "tensor")
    return jax.shard_map(
        on_device, mesh=mesh, in_specs=in_specs, out_specs=out_specs, check_vma=False
    )
```

```python
import functools
import math

import jax
import jax.numpy as jnp
from jax import lax
from jax.experimental import pallas as pl
from jax.experimental.pallas import tpu as pltpu
from jax.sharding import PartitionSpec as P

HEAD = 128
SPAN = 64
NBLEN = 64
KN = 2


MESH = pl.DeviceIdType.MESH
SIDE = 4
CORES = 2
HEADS = 2


class Link:
    def __init__(self, send_sem, recv_sem):
        self.send_sem, self.recv_sem, self.sent = send_sem, recv_sem, []

    def send(self, src, dst, device):
        n = len(self.sent)
        copy = pltpu.make_async_remote_copy(
            src_ref=src,
            dst_ref=dst,
            send_sem=self.send_sem.at[n],
            recv_sem=self.recv_sem.at[n],
            device_id=device,
            device_id_type=MESH,
        )
        copy.start()
        self.sent.append(copy)
        return copy


class Gather:
    def __init__(self, link, own, out):
        self.link, self.own, self.out = link, own, out
        self.y, self.x, self.k, self.t = place()
        self.copies, self.aside, self.first = {}, [], {}

    def device(self, half, first, second, core=None):
        x, y = (first, second) if half == 0 else (second, first)
        return dp_index(self.x + x, self.y + y, self.k if core is None else core), self.t

    def at(self, half, first, second, item, count):
        x, y = (first, second) if half == 0 else (second, first)
        block = dp_index(self.x + x + SIDE, self.y + y + SIDE, self.k)
        return self.out.at[pl.ds(block * 4 + half * 2 + item, count)]

    def source(self, half, block, item, count):
        if self.own is not None and block == (0, 0):
            return self.own.at[pl.ds(half * 2 + item, count)]
        return self.at(half, *block, item, count)

    def to(self, half, name, block, item, count):
        way = {"P+": (1, 0), "P-": (-1, 0), "S+": (0, 1), "S-": (0, -1)}[name[:2]]
        self.copies[half, name] = self.link.send(
            self.source(half, block, item, count),
            self.at(half, *block, item, count),
            self.device(half, *way),
        )

    def side(self, half, block, item, count):
        self.aside.append(
            self.link.send(
                self.source(half, block, item, count),
                self.at(half, *block, item, count),
                self.device(half, 0, 0, 1 - self.k),
            )
        )

    def got(self, half, name, block, item, count):
        self.copies[half, name].wait_recv()
        self.side(half, block, item, count)

    def start(self, h, item, count):
        for way in ("P+", "P-", "S+", "S-"):
            self.to(h, f"{way} {item}", (0, 0), item, count)
        self.side(h, (0, 0), item, count)
        self.first.setdefault(h, []).append((item, count))

    def arrived(self, h, way, block):
        for item, count in self.first[h]:
            self.got(h, f"{way} {item}", block, item, count)

    def second(self, h):
        self.arrived(h, "P+", (-1, 0))
        self.to(h, "P+f", (-1, 0), 0, 1)
        self.to(h, "S+l", (-1, 0), 0, 2)
        self.to(h, "S-l", (-1, 0), 0, 2)
        self.arrived(h, "P-", (1, 0))
        self.to(h, "P-f", (1, 0), 1, 1)
        self.to(h, "S+r", (1, 0), 0, 2)
        self.to(h, "S-r", (1, 0), 0, 2)
        self.arrived(h, "S+", (0, -1))
        self.to(h, "S+f", (0, -1), 0, 1)
        self.arrived(h, "S-", (0, 1))
        self.to(h, "S-f", (0, 1), 1, 1)

    def third(self, h):
        self.got(h, "P+f", (-2, 0), 0, 1)
        self.to(h, "S+0", (-2, 0), 0, 1)
        self.to(h, "S-0", (-2, 0), 0, 1)
        self.got(h, "P-f", (2, 0), 1, 1)
        self.to(h, "S+1", (2, 0), 1, 1)
        self.to(h, "S-1", (2, 0), 1, 1)
        self.got(h, "S+l", (-1, -1), 0, 2)
        self.to(h, "S+lf", (-1, -1), 0, 1)
        self.got(h, "S-l", (-1, 1), 0, 2)
        self.to(h, "S-lf", (-1, 1), 1, 1)
        self.got(h, "S+r", (1, -1), 0, 2)
        self.to(h, "S+rf", (1, -1), 0, 1)
        self.got(h, "S-r", (1, 1), 0, 2)
        self.to(h, "S-rf", (1, 1), 1, 1)
        self.got(h, "S+f", (0, -2), 0, 1)
        self.got(h, "S-f", (0, 2), 1, 1)

    def fourth(self, h):
        self.got(h, "S+0", (-2, -1), 0, 1)
        self.to(h, "S+0f", (-2, -1), 0, 1)
        self.got(h, "S-1", (2, 1), 1, 1)
        self.to(h, "S-1f", (2, 1), 1, 1)
        self.got(h, "S+1", (2, -1), 1, 1)
        self.got(h, "S-0", (-2, 1), 0, 1)
        self.got(h, "S+lf", (-1, -2), 0, 1)
        self.got(h, "S-lf", (-1, 2), 1, 1)
        self.got(h, "S+rf", (1, -2), 0, 1)
        self.got(h, "S-rf", (1, 2), 1, 1)

    def fifth(self, h):
        self.got(h, "S+0f", (-2, -2), 0, 1)
        self.got(h, "S-1f", (2, 2), 1, 1)

    def finish(self):
        for copy in self.aside:
            copy.wait_recv()


def dp_index(x, y, core):
    return (y % SIDE * SIDE + x % SIDE) * CORES + core


def place():
    me = lax.axis_index("dp")
    return me // (SIDE * CORES), me // CORES % SIDE, me % CORES, lax.axis_index("tensor")


def exchange_kernel(
    scale,
    n_t,
    owner_ref,
    index_ref,
    gain_ref,
    store_ref,
    wq_ref,
    wkv_ref,
    hidden_ref,
    wc_ref,
    wout_ref,
    kv_all_ref,
    c_ref,
    store_v,
    wq_v,
    wkv_v,
    hidden_v,
    wc_v,
    wout_v,
    joined_v,
    kv_own_v,
    q_all_v,
    q_sel_v,
    normed_v,
    far_v,
    up_v,
    down_v,
    own_v,
    far_in_v,
    left_v,
    right_v,
    cond_v,
    ctx_v,
    send_sem,
    recv_sem,
    load_sem,
):
    y, x, core, t = place()
    me = lax.axis_index("dp")
    above, below = (me, (t + 1) % n_t), (me, (t + n_t - 1) % n_t)
    twin = (dp_index(x, y, 1 - core), t)
    stored = store_v.shape[0]
    tile = 2 * HEAD
    tiles = wkv_v.shape[1] // tile
    pairs = q_sel_v.shape[0]
    spans = pairs // KN

    loads = [
        pltpu.make_async_copy(src, dst, load_sem.at[n])
        for n, (src, dst) in enumerate(
            (
                (store_ref, store_v),
                (wq_ref, wq_v),
                (wkv_ref, wkv_v),
                (hidden_ref, hidden_v),
                (wc_ref, wc_v),
                (wout_ref, wout_v.at[0]),
            )
        )
    ]
    for load in loads[:3]:
        load.start()
    barrier = pltpu.get_barrier_semaphore()
    beside = [
        (dp_index(x + 1, y, core), t),
        (dp_index(x + SIDE - 1, y, core), t),
        (dp_index(x, y + 1, core), t),
        (dp_index(x, y + SIDE - 1, core), t),
        twin,
        above,
        below,
    ]
    for device in beside:
        pl.semaphore_signal(barrier, inc=1, device_id=device, device_id_type=MESH)

    link = Link(send_sem, recv_sem)
    q_gather = Gather(link, None, q_all_v)
    kv_gather = Gather(link, kv_own_v, kv_all_ref)

    loads[0].wait()
    gain = gain_ref[...]
    for n in range(stored):
        rows = store_v[n].astype(jnp.float32)
        spread = jnp.mean(rows * rows, axis=-1, keepdims=True)
        normed_v[n] = (rows * lax.rsqrt(spread + 1e-05) * gain).astype(jnp.bfloat16)
    loads[1].wait()
    q_own = (
        jnp.dot(
            normed_v[...].reshape(stored * NBLEN, normed_v.shape[2]),
            wq_v[...],
            preferred_element_type=jnp.float32,
        )
        .astype(jnp.bfloat16)
        .reshape(stored, NBLEN, wq_v.shape[1])
    )
    for half in (0, 1):
        q_gather.at(half, 0, 0, 0, 2)[...] = q_own[2 * half : 2 * half + 2]
    pl.semaphore_wait(barrier, len(beside))
    for half in (0, 1):
        q_gather.start(half, 0, 2)
    w_up = link.send(wout_ref.at[core], wout_v.at[1, core], above)
    w_down = link.send(wout_ref.at[core], wout_v.at[2, core], below)
    loads[2].wait()
    for load in loads[3:]:
        load.start()

    def kv_tile(n, carry):
        columns = pl.ds(pl.multiple_of(n * tile, tile), tile)
        kv_own_v[:, :, columns] = (
            jnp.dot(
                store_v[...].reshape(stored * NBLEN, store_v.shape[2]),
                wkv_v[:, columns],
                preferred_element_type=jnp.float32,
            )
            .astype(jnp.bfloat16)
            .reshape(stored, NBLEN, tile)
        )
        return carry

    lax.fori_loop(0, tiles // 2, kv_tile, 0)
    for half in (0, 1):
        q_gather.second(half)
    lax.fori_loop(tiles // 2, tiles, kv_tile, 0)
    for half in (0, 1):
        q_gather.third(half)
    kv_gather.start(0, 0, 1)
    kept = []
    for half in (0, 1):
        copy = pltpu.make_async_copy(
            kv_own_v.at[pl.ds(2 * half, 2)],
            kv_gather.at(half, 0, 0, 0, 2),
            load_sem.at[len(loads) + half],
        )
        copy.start()
        kept.append(copy)

    loads[3].wait()
    loads[4].wait()

    def part(block, half):
        column = ((t + block) % n_t * 2 + half) * tile
        return jnp.dot(
            hidden_v[...],
            wc_v[:, pl.ds(pl.multiple_of(column, tile), tile)],
            preferred_element_type=jnp.float32,
        )

    far_v[0] = part(2, 0).astype(jnp.bfloat16)
    far_up = link.send(far_v.at[0], far_in_v.at[0], above)
    for half in (0, 1):
        q_gather.fourth(half)
    far_v[1] = part(2, 1).astype(jnp.bfloat16)
    far_down = link.send(far_v.at[1], far_in_v.at[1], below)
    kv_gather.start(0, 1, 1)
    kv_gather.start(1, 0, 1)
    up_v[1] = part(1, 1).astype(jnp.bfloat16)
    near_up = link.send(up_v.at[1], left_v.at[1], above)
    down_v[0] = part(3, 0).astype(jnp.bfloat16)
    near_down = link.send(down_v.at[0], right_v.at[0], below)
    kv_gather.start(1, 1, 1)
    first_up = part(1, 0)
    first_down = part(3, 1)
    far_up.wait_recv()
    up_v[0] = (first_up + far_in_v[0].astype(jnp.float32)).astype(jnp.bfloat16)
    last_up = link.send(up_v.at[0], left_v.at[0], above)
    far_down.wait_recv()
    down_v[1] = (first_down + far_in_v[1].astype(jnp.float32)).astype(jnp.bfloat16)
    last_down = link.send(down_v.at[1], right_v.at[1], below)

    w_up.wait_recv()
    w_far_up = link.send(wout_v.at[1, core, 0], wout_v.at[3, core, 0], above)
    w_aside = [link.send(wout_v.at[1, core], wout_v.at[1, core], twin)]
    w_down.wait_recv()
    w_far_down = link.send(wout_v.at[2, core, 1], wout_v.at[3, core, 1], below)
    w_aside.append(link.send(wout_v.at[2, core], wout_v.at[2, core], twin))
    kv_gather.second(0)
    own_v[0] = part(0, 0)
    own_v[1] = part(0, 1)
    for half in (0, 1):
        q_gather.fifth(half)
    q_gather.finish()

    def pick(c, carry):
        for k in range(KN):
            q_sel_v[KN * c + k] = q_all_v[owner_ref[k, c] * stored + index_ref[k, c]]
        return carry

    lax.fori_loop(0, spans, pick, 0)
    kv_gather.second(1)

    for copy in (near_up, near_down, last_up, last_down):
        copy.wait_recv()
    for h in range(2):
        cond_v[h] = (
            own_v[h] + left_v[h].astype(jnp.float32) + right_v[h].astype(jnp.float32)
        ).astype(jnp.bfloat16)
    for h in range(2):
        query = q_sel_v[:, :, h * HEAD : (h + 1) * HEAD].reshape(spans, KN * NBLEN, HEAD)
        keys = cond_v[h, :, :HEAD].reshape(spans, SPAN, HEAD)
        values = cond_v[h, :, HEAD:].reshape(spans, SPAN, HEAD)
        scores = (
            jnp.einsum("cld,ckd->clk", query, keys, preferred_element_type=jnp.float32) * scale
        )
        weights = jnp.exp(scores - jnp.max(scores, axis=-1, keepdims=True))
        weights = (weights / jnp.sum(weights, axis=-1, keepdims=True)).astype(jnp.bfloat16)
        context = jnp.einsum("clk,ckd->cld", weights, values, preferred_element_type=jnp.float32)
        ctx_v[0, h] = context.astype(jnp.bfloat16).reshape(ctx_v.shape[2], HEAD)
        if h == 0:
            ctx_up = [link.send(ctx_v.at[0, 0], ctx_v.at[1, 0], above)]
    ctx_down = [link.send(ctx_v.at[0, 1], ctx_v.at[2, 1], below)]
    ctx_up.append(link.send(ctx_v.at[0, 1], ctx_v.at[1, 1], above))
    ctx_down.append(link.send(ctx_v.at[0, 0], ctx_v.at[2, 0], below))

    w_far_up.wait_recv()
    w_aside.append(link.send(wout_v.at[3, core, 0], wout_v.at[3, core, 0], twin))
    w_far_down.wait_recv()
    w_aside.append(link.send(wout_v.at[3, core, 1], wout_v.at[3, core, 1], twin))
    loads[5].wait()
    for copy in w_aside:
        copy.wait_recv()

    def joined_tile(n, carry):
        columns = pl.ds(pl.multiple_of(n * tile, tile), tile)
        joined_v[:, columns] = jnp.dot(
            wout_v[...].reshape(joined_v.shape[0], wout_v.shape[4]),
            wkv_v[:, columns],
            preferred_element_type=jnp.float32,
        ).astype(jnp.bfloat16)
        return carry

    lax.fori_loop(0, tiles, joined_tile, 0)

    ctx_up[0].wait_recv()
    ctx_far_up = link.send(ctx_v.at[1, 0], ctx_v.at[3, 0], above)
    ctx_down[0].wait_recv()
    ctx_far_down = link.send(ctx_v.at[2, 1], ctx_v.at[3, 1], below)

    kv_gather.third(0)
    ctx_up[1].wait_recv()
    ctx_down[1].wait_recv()
    rows = ctx_v.shape[2]

    def term(j, columns):
        return jnp.dot(
            jnp.concatenate([ctx_v[j, 0], ctx_v[j, 1]], axis=-1),
            joined_v[j * 2 * HEAD : (j + 1) * 2 * HEAD, columns],
            preferred_element_type=jnp.float32,
        )

    def c_near(n, carry):
        columns = pl.ds(pl.multiple_of(n * tile, tile), tile)
        total = term(0, columns) + term(1, columns) + term(2, columns)
        wc_v[:rows, columns] = total.astype(jnp.bfloat16)
        return carry

    def c_far(n, carry):
        columns = pl.ds(pl.multiple_of(n * tile, tile), tile)
        total = wc_v[:rows, columns].astype(jnp.float32) + term(3, columns)
        wc_v[:rows, columns] = total.astype(jnp.bfloat16)
        return carry

    lax.fori_loop(0, tiles // 2, c_near, 0)
    kv_gather.third(1)
    lax.fori_loop(tiles // 2, tiles, c_near, 0)
    ctx_far_up.wait_recv()
    ctx_far_down.wait_recv()
    lax.fori_loop(0, tiles, c_far, 0)
    out = pltpu.make_async_copy(wc_v.at[pl.ds(0, rows)], c_ref, load_sem.at[len(loads) + 2])
    out.start()
    for half in (0, 1):
        kv_gather.fourth(half)
    for half in (0, 1):
        kv_gather.fifth(half)
    kv_gather.finish()
    out.wait()
    for copy in kept:
        copy.wait()
    for copy in link.sent:
        copy.wait_send()


def decoder_kernel(scale, pairs, owner_ref, index_ref, count_ref, *refs):
    stored_refs = refs[:pairs]
    c_ref, q_ref, out_ref = refs[pairs:]
    key_place = lax.broadcasted_iota(jnp.int32, (SPAN, KN * NBLEN), 1) // NBLEN
    spans = pairs // KN
    for g in range(q_ref.shape[1] // HEAD):
        columns = slice(2 * g * HEAD, (2 * g + 2) * HEAD)
        head = slice(g * HEAD, (g + 1) * HEAD)
        all_scores = []
        all_values = []
        for c in range(spans):
            stored = jnp.concatenate(
                [stored_refs[KN * c + k][0, :, columns] for k in range(KN)], axis=0
            )
            here = (
                c_ref[c * KN * NBLEN : (c + 1) * KN * NBLEN, columns].astype(jnp.float32)
                + stored.astype(jnp.float32)
            ).astype(jnp.bfloat16)
            all_values.append(here[:, HEAD:])
            scores = (
                lax.dot_general(
                    q_ref[c * SPAN : (c + 1) * SPAN, head],
                    here[:, :HEAD],
                    (((1,), (1,)), ((), ())),
                    preferred_element_type=jnp.float32,
                )
                * scale
            )
            all_scores.append(jnp.where(key_place < count_ref[c], scores, jnp.float32(-1e30)))
        for c in range(spans):
            scores = all_scores[c]
            weights = jnp.exp(scores - jnp.max(scores, axis=-1, keepdims=True))
            weights = (weights / jnp.sum(weights, axis=-1, keepdims=True)).astype(jnp.bfloat16)
            out_ref[c * SPAN : (c + 1) * SPAN, head] = jnp.dot(
                weights, all_values[c], preferred_element_type=jnp.float32
            ).astype(jnp.bfloat16)


def on_device(
    dec_hidden,
    dec_query,
    store,
    norm_gain,
    w_query_enc,
    w_cond,
    w_out_enc,
    w_kv_dec,
    owner,
    nb_index,
    nb_count,
):
    scale = 1.0 / math.sqrt(HEAD)
    n_t = lax.axis_size("tensor")
    tokens = dec_hidden.shape[0]
    spans = tokens // SPAN
    pairs = spans * KN
    rows = pairs * NBLEN
    stored, _, width_e = store.shape
    width_q = w_query_enc.shape[1]
    width_kv = w_kv_dec.shape[1]
    owner_t, index_t = owner.T, nb_index.T
    bf16, f32 = jnp.bfloat16, jnp.float32
    quarter = w_out_enc.shape[0] // 4
    half_c = 2 * HEAD
    anywhere = pl.BlockSpec(memory_space=pl.ANY)
    copies = 2 * 90 + 20 + 8 + 6 + 6
    kv_all, extra = pl.pallas_call(
        functools.partial(exchange_kernel, scale, n_t),
        out_shape=(
            jax.ShapeDtypeStruct((lax.axis_size("dp") * stored, NBLEN, width_kv), bf16),
            jax.ShapeDtypeStruct((rows, width_kv), bf16),
        ),
        in_specs=[
            pl.BlockSpec(memory_space=pltpu.SMEM),
            pl.BlockSpec(memory_space=pltpu.SMEM),
            pl.BlockSpec(memory_space=pltpu.VMEM),
        ]
        + [anywhere] * 6,
        out_specs=(anywhere, anywhere),
        scratch_shapes=[
            pltpu.VMEM((stored, NBLEN, width_e), bf16),
            pltpu.VMEM(w_query_enc.shape, bf16),
            pltpu.VMEM(w_kv_dec.shape, bf16),
            pltpu.VMEM(dec_hidden.shape, bf16),
            pltpu.VMEM(w_cond.shape, bf16),
            pltpu.VMEM((n_t, 2, 2, quarter, width_e), bf16),
            pltpu.VMEM((n_t * w_out_enc.shape[0], width_kv), bf16),
            pltpu.VMEM((stored, NBLEN, width_kv), bf16),
            pltpu.VMEM((lax.axis_size("dp") * stored, NBLEN, width_q), bf16),
            pltpu.VMEM((pairs, NBLEN, width_q), bf16),
            pltpu.VMEM((stored, NBLEN, width_e), bf16),
            pltpu.VMEM((2, tokens, half_c), bf16),
            pltpu.VMEM((2, tokens, half_c), bf16),
            pltpu.VMEM((2, tokens, half_c), bf16),
            pltpu.VMEM((2, tokens, half_c), f32),
            pltpu.VMEM((2, tokens, half_c), bf16),
            pltpu.VMEM((2, tokens, half_c), bf16),
            pltpu.VMEM((2, tokens, half_c), bf16),
            pltpu.VMEM((2, tokens, half_c), bf16),
            pltpu.VMEM((n_t, 2, rows, HEAD), bf16),
            pltpu.SemaphoreType.DMA((copies,)),
            pltpu.SemaphoreType.DMA((copies,)),
            pltpu.SemaphoreType.DMA((9,)),
        ],
        compiler_params=pltpu.CompilerParams(
            collective_id=0, has_side_effects=True, vmem_limit_bytes=60 << 20
        ),
        name="exchange",
    )(
        owner_t,
        index_t,
        norm_gain.reshape(1, width_e),
        store,
        w_query_enc,
        w_kv_dec,
        dec_hidden,
        w_cond,
        w_out_enc.reshape(2, 2, quarter, width_e),
    )

    heads_width = dec_query.shape[1]
    return pl.pallas_call(
        functools.partial(decoder_kernel, scale, pairs),
        out_shape=jax.ShapeDtypeStruct((tokens, heads_width), bf16),
        grid_spec=pltpu.PrefetchScalarGridSpec(
            num_scalar_prefetch=3,
            grid=(heads_width // (HEADS * HEAD),),
            in_specs=[
                pl.BlockSpec(
                    (1, NBLEN, 2 * HEADS * HEAD),
                    lambda g, own, idx, count, c=p // KN, k=p % KN: (
                        own[k, c] * stored + idx[k, c],
                        0,
                        g,
                    ),
                )
                for p in range(pairs)
            ]
            + [
                pl.BlockSpec((rows, 2 * HEADS * HEAD), lambda g, own, idx, count: (0, g)),
                pl.BlockSpec((tokens, HEADS * HEAD), lambda g, own, idx, count: (0, g)),
            ],
            out_specs=pl.BlockSpec((tokens, HEADS * HEAD), lambda g, own, idx, count: (0, g)),
        ),
        compiler_params=pltpu.CompilerParams(vmem_limit_bytes=56 << 20),
        name="decoder_attention",
    )(owner_t, index_t, nb_count, *([kv_all] * pairs), extra, dec_query)


def solution(mesh):
    in_specs = (
        P("dp", "tensor"),
        P("dp", "tensor"),
        P("dp", None, None),
        P(),
        P(None, "tensor"),
        P("tensor", None),
        P("tensor", None),
        P(None, "tensor"),
        P("dp", None),
        P("dp", None),
        P("dp"),
    )
    out_specs = P("dp", "tensor")
    return jax.shard_map(
        on_device, mesh=mesh, in_specs=in_specs, out_specs=out_specs, check_vma=False
    )
```

```python
import functools
import math

import jax
import jax.numpy as jnp
from jax import lax
from jax.experimental import pallas as pl
from jax.experimental.pallas import tpu as pltpu
from jax.sharding import PartitionSpec as P

HEAD = 128
SPAN = 64
NBLEN = 64
KN = 2


MESH = pl.DeviceIdType.MESH
SIDE = 4
CORES = 2
HEADS = 2


class Link:
    def __init__(self, send_sem, recv_sem):
        self.send_sem, self.recv_sem, self.sent = send_sem, recv_sem, []

    def send(self, src, dst, device):
        n = len(self.sent)
        copy = pltpu.make_async_remote_copy(
            src_ref=src,
            dst_ref=dst,
            send_sem=self.send_sem.at[n],
            recv_sem=self.recv_sem.at[n],
            device_id=device,
            device_id_type=MESH,
        )
        copy.start()
        self.sent.append(copy)
        return copy


class Gather:
    def __init__(self, link, own, out):
        self.link, self.own, self.out = link, own, out
        self.y, self.x, self.k, self.t = place()
        self.copies, self.aside, self.first = {}, [], {}

    def device(self, half, first, second, core=None):
        x, y = (first, second) if half == 0 else (second, first)
        return dp_index(self.x + x, self.y + y, self.k if core is None else core), self.t

    def at(self, half, first, second, item, count):
        x, y = (first, second) if half == 0 else (second, first)
        block = dp_index(self.x + x + SIDE, self.y + y + SIDE, self.k)
        return self.out.at[pl.ds(block * 4 + half * 2 + item, count)]

    def source(self, half, block, item, count):
        if self.own is not None and block == (0, 0):
            return self.own.at[pl.ds(half * 2 + item, count)]
        return self.at(half, *block, item, count)

    def to(self, half, name, block, item, count):
        way = {"P+": (1, 0), "P-": (-1, 0), "S+": (0, 1), "S-": (0, -1)}[name[:2]]
        self.copies[half, name] = self.link.send(
            self.source(half, block, item, count),
            self.at(half, *block, item, count),
            self.device(half, *way),
        )

    def side(self, half, block, item, count):
        self.aside.append(
            self.link.send(
                self.source(half, block, item, count),
                self.at(half, *block, item, count),
                self.device(half, 0, 0, 1 - self.k),
            )
        )

    def got(self, half, name, block, item, count):
        self.copies[half, name].wait_recv()
        self.side(half, block, item, count)

    def start(self, h, item, count):
        for way in ("P+", "P-", "S+", "S-"):
            self.to(h, f"{way} {item}", (0, 0), item, count)
        self.side(h, (0, 0), item, count)
        self.first.setdefault(h, []).append((item, count))

    def arrived(self, h, way, block):
        for item, count in self.first[h]:
            self.got(h, f"{way} {item}", block, item, count)

    def second(self, h):
        self.arrived(h, "P+", (-1, 0))
        self.to(h, "P+f", (-1, 0), 0, 1)
        self.to(h, "S+l", (-1, 0), 0, 2)
        self.to(h, "S-l", (-1, 0), 0, 2)
        self.arrived(h, "P-", (1, 0))
        self.to(h, "P-f", (1, 0), 1, 1)
        self.to(h, "S+r", (1, 0), 0, 2)
        self.to(h, "S-r", (1, 0), 0, 2)
        self.arrived(h, "S+", (0, -1))
        self.to(h, "S+f", (0, -1), 0, 1)
        self.arrived(h, "S-", (0, 1))
        self.to(h, "S-f", (0, 1), 1, 1)

    def third(self, h):
        self.got(h, "P+f", (-2, 0), 0, 1)
        self.to(h, "S+0", (-2, 0), 0, 1)
        self.to(h, "S-0", (-2, 0), 0, 1)
        self.got(h, "P-f", (2, 0), 1, 1)
        self.to(h, "S+1", (2, 0), 1, 1)
        self.to(h, "S-1", (2, 0), 1, 1)
        self.got(h, "S+l", (-1, -1), 0, 2)
        self.to(h, "S+lf", (-1, -1), 0, 1)
        self.got(h, "S-l", (-1, 1), 0, 2)
        self.to(h, "S-lf", (-1, 1), 1, 1)
        self.got(h, "S+r", (1, -1), 0, 2)
        self.to(h, "S+rf", (1, -1), 0, 1)
        self.got(h, "S-r", (1, 1), 0, 2)
        self.to(h, "S-rf", (1, 1), 1, 1)
        self.got(h, "S+f", (0, -2), 0, 1)
        self.got(h, "S-f", (0, 2), 1, 1)

    def fourth(self, h):
        self.got(h, "S+0", (-2, -1), 0, 1)
        self.to(h, "S+0f", (-2, -1), 0, 1)
        self.got(h, "S-1", (2, 1), 1, 1)
        self.to(h, "S-1f", (2, 1), 1, 1)
        self.got(h, "S+1", (2, -1), 1, 1)
        self.got(h, "S-0", (-2, 1), 0, 1)
        self.got(h, "S+lf", (-1, -2), 0, 1)
        self.got(h, "S-lf", (-1, 2), 1, 1)
        self.got(h, "S+rf", (1, -2), 0, 1)
        self.got(h, "S-rf", (1, 2), 1, 1)

    def fifth(self, h):
        self.got(h, "S+0f", (-2, -2), 0, 1)
        self.got(h, "S-1f", (2, 2), 1, 1)

    def finish(self):
        for copy in self.aside:
            copy.wait_recv()


def dp_index(x, y, core):
    return (y % SIDE * SIDE + x % SIDE) * CORES + core


def place():
    me = lax.axis_index("dp")
    return me // (SIDE * CORES), me // CORES % SIDE, me % CORES, lax.axis_index("tensor")


def exchange_kernel(
    scale,
    n_t,
    owner_ref,
    index_ref,
    gain_ref,
    store_ref,
    wq_ref,
    wkv_ref,
    hidden_ref,
    wc_ref,
    wout_ref,
    kv_all_ref,
    c_ref,
    store_v,
    wq_v,
    wkv_v,
    hidden_v,
    wc_v,
    wout_v,
    joined_v,
    kv_own_v,
    q_all_v,
    q_sel_v,
    normed_v,
    far_v,
    up_v,
    down_v,
    own_v,
    far_in_v,
    left_v,
    right_v,
    cond_v,
    ctx_v,
    send_sem,
    recv_sem,
    load_sem,
):
    y, x, core, t = place()
    me = lax.axis_index("dp")
    above, below = (me, (t + 1) % n_t), (me, (t + n_t - 1) % n_t)
    twin = (dp_index(x, y, 1 - core), t)
    stored = store_v.shape[0]
    tile = 2 * HEAD
    tiles = wkv_v.shape[1] // tile
    pairs = q_sel_v.shape[0]
    spans = pairs // KN

    loads = [
        pltpu.make_async_copy(src, dst, load_sem.at[n])
        for n, (src, dst) in enumerate(
            (
                (store_ref, store_v),
                (wq_ref, wq_v),
                (wkv_ref, wkv_v),
                (hidden_ref, hidden_v),
                (wc_ref, wc_v),
                (wout_ref, wout_v.at[0]),
            )
        )
    ]
    for load in loads[:3]:
        load.start()
    barrier = pltpu.get_barrier_semaphore()
    beside = [
        (dp_index(x + 1, y, core), t),
        (dp_index(x + SIDE - 1, y, core), t),
        (dp_index(x, y + 1, core), t),
        (dp_index(x, y + SIDE - 1, core), t),
        twin,
        above,
        below,
    ]
    for device in beside:
        pl.semaphore_signal(barrier, inc=1, device_id=device, device_id_type=MESH)

    link = Link(send_sem, recv_sem)
    q_gather = Gather(link, None, q_all_v)
    kv_gather = Gather(link, kv_own_v, kv_all_ref)

    loads[0].wait()
    gain = gain_ref[...]
    for n in range(stored):
        rows = store_v[n].astype(jnp.float32)
        spread = jnp.mean(rows * rows, axis=-1, keepdims=True)
        normed_v[n] = (rows * lax.rsqrt(spread + 1e-05) * gain).astype(jnp.bfloat16)
    loads[1].wait()
    q_own = (
        jnp.dot(
            normed_v[...].reshape(stored * NBLEN, normed_v.shape[2]),
            wq_v[...],
            preferred_element_type=jnp.float32,
        )
        .astype(jnp.bfloat16)
        .reshape(stored, NBLEN, wq_v.shape[1])
    )
    for half in (0, 1):
        q_gather.at(half, 0, 0, 0, 2)[...] = q_own[2 * half : 2 * half + 2]
    pl.semaphore_wait(barrier, len(beside))
    for half in (0, 1):
        q_gather.start(half, 0, 2)
    w_up = link.send(wout_ref.at[core], wout_v.at[1, core], above)
    w_down = link.send(wout_ref.at[core], wout_v.at[2, core], below)
    loads[2].wait()
    for load in loads[3:]:
        load.start()

    def kv_tile(n, carry):
        columns = pl.ds(pl.multiple_of(n * tile, tile), tile)
        kv_own_v[:, :, columns] = (
            jnp.dot(
                store_v[...].reshape(stored * NBLEN, store_v.shape[2]),
                wkv_v[:, columns],
                preferred_element_type=jnp.float32,
            )
            .astype(jnp.bfloat16)
            .reshape(stored, NBLEN, tile)
        )
        return carry

    lax.fori_loop(0, tiles // 2, kv_tile, 0)
    for half in (0, 1):
        q_gather.second(half)
    lax.fori_loop(tiles // 2, tiles, kv_tile, 0)
    for half in (0, 1):
        q_gather.third(half)
    kv_gather.start(0, 0, 1)
    kv_gather.start(0, 1, 1)
    kept = []
    for half in (0, 1):
        copy = pltpu.make_async_copy(
            kv_own_v.at[pl.ds(2 * half, 2)],
            kv_gather.at(half, 0, 0, 0, 2),
            load_sem.at[len(loads) + half],
        )
        copy.start()
        kept.append(copy)

    loads[3].wait()
    loads[4].wait()

    def part(block, half):
        column = ((t + block) % n_t * 2 + half) * tile
        return jnp.dot(
            hidden_v[...],
            wc_v[:, pl.ds(pl.multiple_of(column, tile), tile)],
            preferred_element_type=jnp.float32,
        )

    far_v[0] = part(2, 0).astype(jnp.bfloat16)
    far_up = link.send(far_v.at[0], far_in_v.at[0], above)
    for half in (0, 1):
        q_gather.fourth(half)
    far_v[1] = part(2, 1).astype(jnp.bfloat16)
    far_down = link.send(far_v.at[1], far_in_v.at[1], below)
    kv_gather.start(1, 0, 1)
    kv_gather.start(1, 1, 1)
    up_v[1] = part(1, 1).astype(jnp.bfloat16)
    near_up = link.send(up_v.at[1], left_v.at[1], above)
    down_v[0] = part(3, 0).astype(jnp.bfloat16)
    near_down = link.send(down_v.at[0], right_v.at[0], below)
    first_up = part(1, 0)
    first_down = part(3, 1)
    own_v[0] = part(0, 0)
    own_v[1] = part(0, 1)
    kv_gather.second(0)
    far_up.wait_recv()
    up_v[0] = (first_up + far_in_v[0].astype(jnp.float32)).astype(jnp.bfloat16)
    last_up = link.send(up_v.at[0], left_v.at[0], above)
    far_down.wait_recv()
    down_v[1] = (first_down + far_in_v[1].astype(jnp.float32)).astype(jnp.bfloat16)
    last_down = link.send(down_v.at[1], right_v.at[1], below)

    w_up.wait_recv()
    w_far_up = link.send(wout_v.at[1, core, 0], wout_v.at[3, core, 0], above)
    w_aside = [link.send(wout_v.at[1, core], wout_v.at[1, core], twin)]
    w_down.wait_recv()
    w_far_down = link.send(wout_v.at[2, core, 1], wout_v.at[3, core, 1], below)
    w_aside.append(link.send(wout_v.at[2, core], wout_v.at[2, core], twin))
    for half in (0, 1):
        q_gather.fifth(half)
    q_gather.finish()

    def pick(c, carry):
        for k in range(KN):
            q_sel_v[KN * c + k] = q_all_v[owner_ref[k, c] * stored + index_ref[k, c]]
        return carry

    lax.fori_loop(0, spans, pick, 0)
    kv_gather.second(1)

    for copy in (near_up, near_down, last_up, last_down):
        copy.wait_recv()
    for h in range(2):
        cond_v[h] = (
            own_v[h] + left_v[h].astype(jnp.float32) + right_v[h].astype(jnp.float32)
        ).astype(jnp.bfloat16)
    for h in range(2):
        query = q_sel_v[:, :, h * HEAD : (h + 1) * HEAD].reshape(spans, KN * NBLEN, HEAD)
        keys = cond_v[h, :, :HEAD].reshape(spans, SPAN, HEAD)
        values = cond_v[h, :, HEAD:].reshape(spans, SPAN, HEAD)
        scores = (
            jnp.einsum("cld,ckd->clk", query, keys, preferred_element_type=jnp.float32) * scale
        )
        weights = jnp.exp(scores - jnp.max(scores, axis=-1, keepdims=True))
        weights = (weights / jnp.sum(weights, axis=-1, keepdims=True)).astype(jnp.bfloat16)
        context = jnp.einsum("clk,ckd->cld", weights, values, preferred_element_type=jnp.float32)
        ctx_v[0, h] = context.astype(jnp.bfloat16).reshape(ctx_v.shape[2], HEAD)
        if h == 0:
            ctx_up = [link.send(ctx_v.at[0, 0], ctx_v.at[1, 0], above)]
    ctx_down = [link.send(ctx_v.at[0, 1], ctx_v.at[2, 1], below)]
    ctx_up.append(link.send(ctx_v.at[0, 1], ctx_v.at[1, 1], above))
    ctx_down.append(link.send(ctx_v.at[0, 0], ctx_v.at[2, 0], below))

    w_far_up.wait_recv()
    w_aside.append(link.send(wout_v.at[3, core, 0], wout_v.at[3, core, 0], twin))
    w_far_down.wait_recv()
    w_aside.append(link.send(wout_v.at[3, core, 1], wout_v.at[3, core, 1], twin))
    loads[5].wait()
    for copy in w_aside:
        copy.wait_recv()

    def joined_tile(n, carry):
        columns = pl.ds(pl.multiple_of(n * tile, tile), tile)
        joined_v[:, columns] = jnp.dot(
            wout_v[...].reshape(joined_v.shape[0], wout_v.shape[4]),
            wkv_v[:, columns],
            preferred_element_type=jnp.float32,
        ).astype(jnp.bfloat16)
        return carry

    lax.fori_loop(0, tiles, joined_tile, 0)

    ctx_up[0].wait_recv()
    ctx_far_up = link.send(ctx_v.at[1, 0], ctx_v.at[3, 0], above)
    ctx_down[0].wait_recv()
    ctx_far_down = link.send(ctx_v.at[2, 1], ctx_v.at[3, 1], below)

    kv_gather.third(0)
    ctx_up[1].wait_recv()
    ctx_down[1].wait_recv()
    rows = ctx_v.shape[2]

    def term(j, columns):
        return jnp.dot(
            jnp.concatenate([ctx_v[j, 0], ctx_v[j, 1]], axis=-1),
            joined_v[j * 2 * HEAD : (j + 1) * 2 * HEAD, columns],
            preferred_element_type=jnp.float32,
        )

    def c_near(n, carry):
        columns = pl.ds(pl.multiple_of(n * tile, tile), tile)
        total = term(0, columns) + term(1, columns) + term(2, columns)
        wc_v[:rows, columns] = total.astype(jnp.bfloat16)
        return carry

    def c_far(n, carry):
        columns = pl.ds(pl.multiple_of(n * tile, tile), tile)
        total = wc_v[:rows, columns].astype(jnp.float32) + term(3, columns)
        wc_v[:rows, columns] = total.astype(jnp.bfloat16)
        return carry

    lax.fori_loop(0, tiles // 2, c_near, 0)
    kv_gather.third(1)
    lax.fori_loop(tiles // 2, tiles, c_near, 0)
    ctx_far_up.wait_recv()
    ctx_far_down.wait_recv()
    lax.fori_loop(0, tiles, c_far, 0)
    out = pltpu.make_async_copy(wc_v.at[pl.ds(0, rows)], c_ref, load_sem.at[len(loads) + 2])
    out.start()
    for half in (0, 1):
        kv_gather.fourth(half)
    for half in (0, 1):
        kv_gather.fifth(half)
    kv_gather.finish()
    out.wait()
    for copy in kept:
        copy.wait()
    for copy in link.sent:
        copy.wait_send()


def decoder_kernel(
    scale,
    stored,
    owner_ref,
    index_ref,
    count_ref,
    kv_ref,
    c_ref,
    q_ref,
    out_ref,
    kv_v,
    c_v,
    q_v,
    out_v,
    in_sem,
    out_sem,
):
    pairs = kv_v.shape[0]
    spans = pairs // KN
    groups = in_sem.shape[0]
    width = HEADS * HEAD
    key_place = lax.broadcasted_iota(jnp.int32, (SPAN, KN * NBLEN), 1) // NBLEN
    ones = jnp.ones((KN * NBLEN, HEAD), jnp.bfloat16)

    def part(n, size):
        return pl.ds(pl.multiple_of(n * size, size), size)

    def fetches(n):
        wide, narrow = part(n, 2 * width), part(n, width)
        copies = []
        for p in range(pairs):
            row = owner_ref[p % KN, p // KN] * stored + index_ref[p % KN, p // KN]
            copies.append(
                pltpu.make_async_copy(
                    kv_ref.at[row, :, wide], kv_v.at[p, :, wide], in_sem.at[n, p]
                )
            )
        copies.append(
            pltpu.make_async_copy(c_ref.at[:, wide], c_v.at[:, wide], in_sem.at[n, pairs])
        )
        copies.append(
            pltpu.make_async_copy(q_ref.at[:, narrow], q_v.at[:, narrow], in_sem.at[n, pairs + 1])
        )
        return copies

    def result(n):
        narrow = part(n, width)
        return pltpu.make_async_copy(out_v.at[:, narrow], out_ref.at[:, narrow], out_sem.at[n])

    def start(n, carry):
        for copy in fetches(n):
            copy.start()
        return carry

    def attend(n, carry):
        for copy in fetches(n):
            copy.wait()
        for g in range(HEADS):
            columns, head = part(n * HEADS + g, 2 * HEAD), part(n * HEADS + g, HEAD)
            all_scores = []
            all_values = []
            for c in range(spans):
                stored_kv = kv_v[KN * c : KN * (c + 1), :, columns].reshape(KN * NBLEN, 2 * HEAD)
                here = (
                    c_v[c * KN * NBLEN : (c + 1) * KN * NBLEN, columns].astype(jnp.float32)
                    + stored_kv.astype(jnp.float32)
                ).astype(jnp.bfloat16)
                all_values.append(here[:, HEAD:])
                scores = (
                    lax.dot_general(
                        q_v[c * SPAN : (c + 1) * SPAN, head],
                        here[:, :HEAD],
                        (((1,), (1,)), ((), ())),
                        preferred_element_type=jnp.float32,
                    )
                    * scale
                )
                all_scores.append(jnp.where(key_place < count_ref[c], scores, jnp.float32(-1e30)))
            for c in range(spans):
                scores = all_scores[c]
                weights = jnp.exp(scores - jnp.max(scores, axis=-1, keepdims=True)).astype(
                    jnp.bfloat16
                )
                total = jnp.dot(weights, ones, preferred_element_type=jnp.float32)
                mixed = jnp.dot(weights, all_values[c], preferred_element_type=jnp.float32)
                out_v[c * SPAN : (c + 1) * SPAN, head] = (mixed / total).astype(jnp.bfloat16)
        result(n).start()
        return carry

    def end(n, carry):
        result(n).wait()
        return carry

    lax.fori_loop(0, groups, start, 0)
    lax.fori_loop(0, groups, attend, 0)
    lax.fori_loop(0, groups, end, 0)


def on_device(
    dec_hidden,
    dec_query,
    store,
    norm_gain,
    w_query_enc,
    w_cond,
    w_out_enc,
    w_kv_dec,
    owner,
    nb_index,
    nb_count,
):
    scale = 1.0 / math.sqrt(HEAD)
    n_t = lax.axis_size("tensor")
    tokens = dec_hidden.shape[0]
    spans = tokens // SPAN
    pairs = spans * KN
    rows = pairs * NBLEN
    stored, _, width_e = store.shape
    width_q = w_query_enc.shape[1]
    width_kv = w_kv_dec.shape[1]
    owner_t, index_t = owner.T, nb_index.T
    bf16, f32 = jnp.bfloat16, jnp.float32
    quarter = w_out_enc.shape[0] // 4
    half_c = 2 * HEAD
    anywhere = pl.BlockSpec(memory_space=pl.ANY)
    copies = 2 * 90 + 20 + 8 + 6 + 6
    kv_all, extra = pl.pallas_call(
        functools.partial(exchange_kernel, scale, n_t),
        out_shape=(
            jax.ShapeDtypeStruct((lax.axis_size("dp") * stored, NBLEN, width_kv), bf16),
            jax.ShapeDtypeStruct((rows, width_kv), bf16),
        ),
        in_specs=[
            pl.BlockSpec(memory_space=pltpu.SMEM),
            pl.BlockSpec(memory_space=pltpu.SMEM),
            pl.BlockSpec(memory_space=pltpu.VMEM),
        ]
        + [anywhere] * 6,
        out_specs=(anywhere, anywhere),
        scratch_shapes=[
            pltpu.VMEM((stored, NBLEN, width_e), bf16),
            pltpu.VMEM(w_query_enc.shape, bf16),
            pltpu.VMEM(w_kv_dec.shape, bf16),
            pltpu.VMEM(dec_hidden.shape, bf16),
            pltpu.VMEM(w_cond.shape, bf16),
            pltpu.VMEM((n_t, 2, 2, quarter, width_e), bf16),
            pltpu.VMEM((n_t * w_out_enc.shape[0], width_kv), bf16),
            pltpu.VMEM((stored, NBLEN, width_kv), bf16),
            pltpu.VMEM((lax.axis_size("dp") * stored, NBLEN, width_q), bf16),
            pltpu.VMEM((pairs, NBLEN, width_q), bf16),
            pltpu.VMEM((stored, NBLEN, width_e), bf16),
            pltpu.VMEM((2, tokens, half_c), bf16),
            pltpu.VMEM((2, tokens, half_c), bf16),
            pltpu.VMEM((2, tokens, half_c), bf16),
            pltpu.VMEM((2, tokens, half_c), f32),
            pltpu.VMEM((2, tokens, half_c), bf16),
            pltpu.VMEM((2, tokens, half_c), bf16),
            pltpu.VMEM((2, tokens, half_c), bf16),
            pltpu.VMEM((2, tokens, half_c), bf16),
            pltpu.VMEM((n_t, 2, rows, HEAD), bf16),
            pltpu.SemaphoreType.DMA((copies,)),
            pltpu.SemaphoreType.DMA((copies,)),
            pltpu.SemaphoreType.DMA((9,)),
        ],
        compiler_params=pltpu.CompilerParams(
            collective_id=0, has_side_effects=True, vmem_limit_bytes=60 << 20
        ),
        name="exchange",
    )(
        owner_t,
        index_t,
        norm_gain.reshape(1, width_e),
        store,
        w_query_enc,
        w_kv_dec,
        dec_hidden,
        w_cond,
        w_out_enc.reshape(2, 2, quarter, width_e),
    )

    heads_width = dec_query.shape[1]
    groups = heads_width // (HEADS * HEAD)
    return pl.pallas_call(
        functools.partial(decoder_kernel, scale, stored),
        out_shape=jax.ShapeDtypeStruct((tokens, heads_width), bf16),
        grid_spec=pltpu.PrefetchScalarGridSpec(
            num_scalar_prefetch=3,
            grid=(1,),
            in_specs=[anywhere] * 3,
            out_specs=anywhere,
            scratch_shapes=[
                pltpu.VMEM((pairs, NBLEN, width_kv), bf16),
                pltpu.VMEM((rows, width_kv), bf16),
                pltpu.VMEM((tokens, heads_width), bf16),
                pltpu.VMEM((tokens, heads_width), bf16),
                pltpu.SemaphoreType.DMA((groups, pairs + 2)),
                pltpu.SemaphoreType.DMA((groups,)),
            ],
        ),
        compiler_params=pltpu.CompilerParams(vmem_limit_bytes=56 << 20),
        name="decoder_attention",
    )(owner_t, index_t, nb_count, kv_all, extra, dec_query)


def solution(mesh):
    in_specs = (
        P("dp", "tensor"),
        P("dp", "tensor"),
        P("dp", None, None),
        P(),
        P(None, "tensor"),
        P("tensor", None),
        P("tensor", None),
        P(None, "tensor"),
        P("dp", None),
        P("dp", None),
        P("dp"),
    )
    out_specs = P("dp", "tensor")
    return jax.shard_map(
        on_device, mesh=mesh, in_specs=in_specs, out_specs=out_specs, check_vma=False
    )
```

```python
import functools
import math

import jax
import jax.numpy as jnp
from jax import lax
from jax.experimental import pallas as pl
from jax.experimental.pallas import tpu as pltpu
from jax.sharding import PartitionSpec as P

HEAD = 128
SPAN = 64
NBLEN = 64
KN = 2


MESH = pl.DeviceIdType.MESH
SIDE = 4
CORES = 2
HEADS = 2


class Link:
    def __init__(self, send_sem, recv_sem):
        self.send_sem, self.recv_sem, self.sent, self.drained = send_sem, recv_sem, [], 0

    def send(self, src, dst, device):
        n = len(self.sent)
        copy = pltpu.make_async_remote_copy(
            src_ref=src,
            dst_ref=dst,
            send_sem=self.send_sem.at[n],
            recv_sem=self.recv_sem.at[n],
            device_id=device,
            device_id_type=MESH,
        )
        copy.start()
        self.sent.append(copy)
        return copy

    def drain(self, upto):
        for copy in self.sent[self.drained : upto]:
            copy.wait_send()
        self.drained = upto


class Gather:
    def __init__(self, link, own, out):
        self.link, self.own, self.out = link, own, out
        self.y, self.x, self.k, self.t = place()
        self.copies, self.aside, self.first = {}, [], {}

    def device(self, half, first, second, core=None):
        x, y = (first, second) if half == 0 else (second, first)
        return dp_index(self.x + x, self.y + y, self.k if core is None else core), self.t

    def at(self, half, first, second, item, count):
        x, y = (first, second) if half == 0 else (second, first)
        block = dp_index(self.x + x + SIDE, self.y + y + SIDE, self.k)
        return self.out.at[pl.ds(block * 4 + half * 2 + item, count)]

    def source(self, half, block, item, count):
        if self.own is not None and block == (0, 0):
            return self.own.at[pl.ds(half * 2 + item, count)]
        return self.at(half, *block, item, count)

    def to(self, half, name, block, item, count):
        way = {"P+": (1, 0), "P-": (-1, 0), "S+": (0, 1), "S-": (0, -1)}[name[:2]]
        self.copies[half, name] = self.link.send(
            self.source(half, block, item, count),
            self.at(half, *block, item, count),
            self.device(half, *way),
        )

    def side(self, half, block, item, count):
        self.aside.append(
            self.link.send(
                self.source(half, block, item, count),
                self.at(half, *block, item, count),
                self.device(half, 0, 0, 1 - self.k),
            )
        )

    def got(self, half, name, block, item, count):
        self.copies[half, name].wait_recv()
        self.side(half, block, item, count)

    def start(self, h, item, count):
        for way in ("P+", "P-", "S+", "S-"):
            self.to(h, f"{way} {item}", (0, 0), item, count)
        self.side(h, (0, 0), item, count)
        self.first.setdefault(h, []).append((item, count))

    def arrived(self, h, way, block):
        for item, count in self.first[h]:
            self.got(h, f"{way} {item}", block, item, count)

    def second(self, h):
        self.arrived(h, "P+", (-1, 0))
        self.to(h, "P+f", (-1, 0), 0, 1)
        self.to(h, "S+l", (-1, 0), 0, 2)
        self.to(h, "S-l", (-1, 0), 0, 2)
        self.arrived(h, "P-", (1, 0))
        self.to(h, "P-f", (1, 0), 1, 1)
        self.to(h, "S+r", (1, 0), 0, 2)
        self.to(h, "S-r", (1, 0), 0, 2)
        self.arrived(h, "S+", (0, -1))
        self.to(h, "S+f", (0, -1), 0, 1)
        self.arrived(h, "S-", (0, 1))
        self.to(h, "S-f", (0, 1), 1, 1)

    def third(self, h):
        self.got(h, "P+f", (-2, 0), 0, 1)
        self.to(h, "S+0", (-2, 0), 0, 1)
        self.to(h, "S-0", (-2, 0), 0, 1)
        self.got(h, "P-f", (2, 0), 1, 1)
        self.to(h, "S+1", (2, 0), 1, 1)
        self.to(h, "S-1", (2, 0), 1, 1)
        self.got(h, "S+l", (-1, -1), 0, 2)
        self.to(h, "S+lf", (-1, -1), 0, 1)
        self.got(h, "S-l", (-1, 1), 0, 2)
        self.to(h, "S-lf", (-1, 1), 1, 1)
        self.got(h, "S+r", (1, -1), 0, 2)
        self.to(h, "S+rf", (1, -1), 0, 1)
        self.got(h, "S-r", (1, 1), 0, 2)
        self.to(h, "S-rf", (1, 1), 1, 1)
        self.got(h, "S+f", (0, -2), 0, 1)
        self.got(h, "S-f", (0, 2), 1, 1)

    def fourth(self, h):
        self.got(h, "S+0", (-2, -1), 0, 1)
        self.to(h, "S+0f", (-2, -1), 0, 1)
        self.got(h, "S-1", (2, 1), 1, 1)
        self.to(h, "S-1f", (2, 1), 1, 1)
        self.got(h, "S+1", (2, -1), 1, 1)
        self.got(h, "S-0", (-2, 1), 0, 1)
        self.got(h, "S+lf", (-1, -2), 0, 1)
        self.got(h, "S-lf", (-1, 2), 1, 1)
        self.got(h, "S+rf", (1, -2), 0, 1)
        self.got(h, "S-rf", (1, 2), 1, 1)

    def fifth(self, h):
        self.got(h, "S+0f", (-2, -2), 0, 1)
        self.got(h, "S-1f", (2, 2), 1, 1)

    def finish(self, upto=None):
        for copy in self.aside[:upto]:
            copy.wait_recv()
        self.aside = self.aside[len(self.aside) if upto is None else upto :]


def dp_index(x, y, core):
    return (y % SIDE * SIDE + x % SIDE) * CORES + core


def place():
    me = lax.axis_index("dp")
    return me // (SIDE * CORES), me // CORES % SIDE, me % CORES, lax.axis_index("tensor")


def exchange_kernel(
    scale,
    n_t,
    owner_ref,
    index_ref,
    gain_ref,
    store_ref,
    wq_ref,
    wkv_ref,
    hidden_ref,
    wc_ref,
    wout_ref,
    kv_all_ref,
    c_ref,
    store_v,
    wq_v,
    wkv_v,
    hidden_v,
    wc_v,
    wout_v,
    joined_v,
    kv_own_v,
    q_all_v,
    q_sel_v,
    normed_v,
    far_v,
    up_v,
    down_v,
    own_v,
    far_in_v,
    left_v,
    right_v,
    cond_v,
    ctx_v,
    send_sem,
    recv_sem,
    load_sem,
):
    y, x, core, t = place()
    me = lax.axis_index("dp")
    above, below = (me, (t + 1) % n_t), (me, (t + n_t - 1) % n_t)
    twin = (dp_index(x, y, 1 - core), t)
    stored = store_v.shape[0]
    tile = 2 * HEAD
    tiles = wkv_v.shape[1] // tile
    pairs = q_sel_v.shape[0]
    spans = pairs // KN

    loads = [
        pltpu.make_async_copy(src, dst, load_sem.at[n])
        for n, (src, dst) in enumerate(
            (
                (store_ref, store_v),
                (wq_ref, wq_v),
                (wkv_ref, wkv_v),
                (hidden_ref, hidden_v),
                (wc_ref, wc_v),
                (wout_ref, wout_v.at[0]),
            )
        )
    ]
    for load in loads[:3]:
        load.start()
    barrier = pltpu.get_barrier_semaphore()
    beside = [
        (dp_index(x + 1, y, core), t),
        (dp_index(x + SIDE - 1, y, core), t),
        (dp_index(x, y + 1, core), t),
        (dp_index(x, y + SIDE - 1, core), t),
        twin,
        above,
        below,
    ]
    for device in beside:
        pl.semaphore_signal(barrier, inc=1, device_id=device, device_id_type=MESH)

    link = Link(send_sem, recv_sem)
    q_gather = Gather(link, None, q_all_v)
    kv_gather = Gather(link, kv_own_v, kv_all_ref)

    loads[0].wait()
    gain = gain_ref[...]
    for n in range(stored):
        rows = store_v[n].astype(jnp.float32)
        spread = jnp.mean(rows * rows, axis=-1, keepdims=True)
        normed_v[n] = (rows * lax.rsqrt(spread + 1e-05) * gain).astype(jnp.bfloat16)
    loads[1].wait()
    q_own = (
        jnp.dot(
            normed_v[...].reshape(stored * NBLEN, normed_v.shape[2]),
            wq_v[...],
            preferred_element_type=jnp.float32,
        )
        .astype(jnp.bfloat16)
        .reshape(stored, NBLEN, wq_v.shape[1])
    )
    for half in (0, 1):
        q_gather.at(half, 0, 0, 0, 2)[...] = q_own[2 * half : 2 * half + 2]
    pl.semaphore_wait(barrier, len(beside))
    for half in (0, 1):
        q_gather.start(half, 0, 2)
    w_up = link.send(wout_ref.at[core], wout_v.at[1, core], above)
    w_down = link.send(wout_ref.at[core], wout_v.at[2, core], below)
    loads[2].wait()
    for load in loads[3:]:
        load.start()

    def kv_tile(n, carry):
        columns = pl.ds(pl.multiple_of(n * tile, tile), tile)
        kv_own_v[:, :, columns] = (
            jnp.dot(
                store_v[...].reshape(stored * NBLEN, store_v.shape[2]),
                wkv_v[:, columns],
                preferred_element_type=jnp.float32,
            )
            .astype(jnp.bfloat16)
            .reshape(stored, NBLEN, tile)
        )
        return carry

    lax.fori_loop(0, tiles // 2, kv_tile, 0)
    for half in (0, 1):
        q_gather.second(half)
    lax.fori_loop(tiles // 2, tiles, kv_tile, 0)
    for half in (0, 1):
        q_gather.third(half)
    kv_gather.start(0, 0, 1)
    kv_gather.start(0, 1, 1)
    kept = []
    for half in (0, 1):
        copy = pltpu.make_async_copy(
            kv_own_v.at[pl.ds(2 * half, 2)],
            kv_gather.at(half, 0, 0, 0, 2),
            load_sem.at[len(loads) + half],
        )
        copy.start()
        kept.append(copy)

    loads[3].wait()
    loads[4].wait()

    def part(block, half):
        column = ((t + block) % n_t * 2 + half) * tile
        return jnp.dot(
            hidden_v[...],
            wc_v[:, pl.ds(pl.multiple_of(column, tile), tile)],
            preferred_element_type=jnp.float32,
        )

    far_v[0] = part(2, 0).astype(jnp.bfloat16)
    far_up = link.send(far_v.at[0], far_in_v.at[0], above)
    for half in (0, 1):
        q_gather.fourth(half)
    far_v[1] = part(2, 1).astype(jnp.bfloat16)
    far_down = link.send(far_v.at[1], far_in_v.at[1], below)
    kv_gather.start(1, 0, 1)
    kv_gather.start(1, 1, 1)
    up_v[1] = part(1, 1).astype(jnp.bfloat16)
    near_up = link.send(up_v.at[1], left_v.at[1], above)
    down_v[0] = part(3, 0).astype(jnp.bfloat16)
    near_down = link.send(down_v.at[0], right_v.at[0], below)
    first_up = part(1, 0)
    first_down = part(3, 1)
    own_v[0] = part(0, 0)
    own_v[1] = part(0, 1)
    kv_gather.second(0)
    far_up.wait_recv()
    up_v[0] = (first_up + far_in_v[0].astype(jnp.float32)).astype(jnp.bfloat16)
    last_up = link.send(up_v.at[0], left_v.at[0], above)
    far_down.wait_recv()
    down_v[1] = (first_down + far_in_v[1].astype(jnp.float32)).astype(jnp.bfloat16)
    last_down = link.send(down_v.at[1], right_v.at[1], below)

    w_up.wait_recv()
    w_far_up = link.send(wout_v.at[1, core, 0], wout_v.at[3, core, 0], above)
    w_aside = [link.send(wout_v.at[1, core], wout_v.at[1, core], twin)]
    w_down.wait_recv()
    w_far_down = link.send(wout_v.at[2, core, 1], wout_v.at[3, core, 1], below)
    w_aside.append(link.send(wout_v.at[2, core], wout_v.at[2, core], twin))
    for half in (0, 1):
        q_gather.fifth(half)
    q_gather.finish()

    def pick(c, carry):
        for k in range(KN):
            q_sel_v[KN * c + k] = q_all_v[owner_ref[k, c] * stored + index_ref[k, c]]
        return carry

    lax.fori_loop(0, spans, pick, 0)
    kv_gather.second(1)

    for copy in (near_up, near_down, last_up, last_down):
        copy.wait_recv()
    for h in range(2):
        cond_v[h] = (
            own_v[h] + left_v[h].astype(jnp.float32) + right_v[h].astype(jnp.float32)
        ).astype(jnp.bfloat16)
    for h in range(2):
        query = q_sel_v[:, :, h * HEAD : (h + 1) * HEAD].reshape(spans, KN * NBLEN, HEAD)
        keys = cond_v[h, :, :HEAD].reshape(spans, SPAN, HEAD)
        values = cond_v[h, :, HEAD:].reshape(spans, SPAN, HEAD)
        scores = (
            jnp.einsum("cld,ckd->clk", query, keys, preferred_element_type=jnp.float32) * scale
        )
        weights = jnp.exp(scores - jnp.max(scores, axis=-1, keepdims=True))
        weights = (weights / jnp.sum(weights, axis=-1, keepdims=True)).astype(jnp.bfloat16)
        context = jnp.einsum("clk,ckd->cld", weights, values, preferred_element_type=jnp.float32)
        ctx_v[0, h] = context.astype(jnp.bfloat16).reshape(ctx_v.shape[2], HEAD)
        if h == 0:
            ctx_up = [link.send(ctx_v.at[0, 0], ctx_v.at[1, 0], above)]
    ctx_down = [link.send(ctx_v.at[0, 1], ctx_v.at[2, 1], below)]
    ctx_up.append(link.send(ctx_v.at[0, 1], ctx_v.at[1, 1], above))
    ctx_down.append(link.send(ctx_v.at[0, 0], ctx_v.at[2, 0], below))

    w_far_up.wait_recv()
    w_aside.append(link.send(wout_v.at[3, core, 0], wout_v.at[3, core, 0], twin))
    w_far_down.wait_recv()
    w_aside.append(link.send(wout_v.at[3, core, 1], wout_v.at[3, core, 1], twin))
    loads[5].wait()
    for copy in w_aside:
        copy.wait_recv()

    def joined_tile(n, carry):
        columns = pl.ds(pl.multiple_of(n * tile, tile), tile)
        joined_v[:, columns] = jnp.dot(
            wout_v[...].reshape(joined_v.shape[0], wout_v.shape[4]),
            wkv_v[:, columns],
            preferred_element_type=jnp.float32,
        ).astype(jnp.bfloat16)
        return carry

    lax.fori_loop(0, tiles, joined_tile, 0)

    ctx_up[0].wait_recv()
    ctx_far_up = link.send(ctx_v.at[1, 0], ctx_v.at[3, 0], above)
    ctx_down[0].wait_recv()
    ctx_far_down = link.send(ctx_v.at[2, 1], ctx_v.at[3, 1], below)

    early, handed = len(link.sent), len(kv_gather.aside)
    kv_gather.third(0)
    ctx_up[1].wait_recv()
    ctx_down[1].wait_recv()
    rows = ctx_v.shape[2]

    def term(j, columns):
        return jnp.dot(
            jnp.concatenate([ctx_v[j, 0], ctx_v[j, 1]], axis=-1),
            joined_v[j * 2 * HEAD : (j + 1) * 2 * HEAD, columns],
            preferred_element_type=jnp.float32,
        )

    def c_near(n, carry):
        columns = pl.ds(pl.multiple_of(n * tile, tile), tile)
        total = term(0, columns) + term(1, columns) + term(2, columns)
        wc_v[:rows, columns] = total.astype(jnp.bfloat16)
        return carry

    def c_far(n, carry):
        columns = pl.ds(pl.multiple_of(n * tile, tile), tile)
        total = wc_v[:rows, columns].astype(jnp.float32) + term(3, columns)
        wc_v[:rows, columns] = total.astype(jnp.bfloat16)
        return carry

    lax.fori_loop(0, tiles // 2, c_near, 0)
    kv_gather.third(1)
    lax.fori_loop(tiles // 2, tiles, c_near, 0)
    ctx_far_up.wait_recv()
    ctx_far_down.wait_recv()
    lax.fori_loop(0, tiles, c_far, 0)
    out = pltpu.make_async_copy(wc_v.at[pl.ds(0, rows)], c_ref, load_sem.at[len(loads) + 2])
    out.start()
    late = len(link.sent)
    for half in (0, 1):
        kv_gather.fourth(half)
    link.drain(early)
    kv_gather.finish(handed)
    out.wait()
    for copy in kept:
        copy.wait()
    for half in (0, 1):
        kv_gather.fifth(half)
    link.drain(late)
    kv_gather.finish()
    link.drain(len(link.sent))


def decoder_kernel(
    scale,
    stored,
    owner_ref,
    index_ref,
    count_ref,
    kv_ref,
    c_ref,
    q_ref,
    out_ref,
    kv_v,
    c_v,
    q_v,
    out_v,
    in_sem,
    out_sem,
):
    pairs = kv_v.shape[0]
    spans = pairs // KN
    groups = in_sem.shape[0]
    width = HEADS * HEAD
    key_place = lax.broadcasted_iota(jnp.int32, (SPAN, KN * NBLEN), 1) // NBLEN
    ones = jnp.ones((KN * NBLEN, HEAD), jnp.bfloat16)

    def part(n, size):
        return pl.ds(pl.multiple_of(n * size, size), size)

    def fetches(n):
        wide, narrow = part(n, 2 * width), part(n, width)
        copies = []
        for p in range(pairs):
            row = owner_ref[p % KN, p // KN] * stored + index_ref[p % KN, p // KN]
            copies.append(
                pltpu.make_async_copy(
                    kv_ref.at[row, :, wide], kv_v.at[p, :, wide], in_sem.at[n, p]
                )
            )
        copies.append(
            pltpu.make_async_copy(c_ref.at[:, wide], c_v.at[:, wide], in_sem.at[n, pairs])
        )
        copies.append(
            pltpu.make_async_copy(q_ref.at[:, narrow], q_v.at[:, narrow], in_sem.at[n, pairs + 1])
        )
        return copies

    def result(n):
        narrow = part(n, width)
        return pltpu.make_async_copy(out_v.at[:, narrow], out_ref.at[:, narrow], out_sem.at[n])

    def start(n, carry):
        for copy in fetches(n):
            copy.start()
        return carry

    def attend(n, carry):
        for copy in fetches(n):
            copy.wait()
        for g in range(HEADS):
            columns, head = part(n * HEADS + g, 2 * HEAD), part(n * HEADS + g, HEAD)
            all_scores = []
            all_values = []
            for c in range(spans):
                stored_kv = kv_v[KN * c : KN * (c + 1), :, columns].reshape(KN * NBLEN, 2 * HEAD)
                here = (
                    c_v[c * KN * NBLEN : (c + 1) * KN * NBLEN, columns].astype(jnp.float32)
                    + stored_kv.astype(jnp.float32)
                ).astype(jnp.bfloat16)
                all_values.append(here[:, HEAD:])
                scores = (
                    lax.dot_general(
                        q_v[c * SPAN : (c + 1) * SPAN, head],
                        here[:, :HEAD],
                        (((1,), (1,)), ((), ())),
                        preferred_element_type=jnp.float32,
                    )
                    * scale
                )
                all_scores.append(jnp.where(key_place < count_ref[c], scores, jnp.float32(-1e30)))
            for c in range(spans):
                scores = all_scores[c]
                weights = jnp.exp(scores - jnp.max(scores, axis=-1, keepdims=True)).astype(
                    jnp.bfloat16
                )
                total = jnp.dot(weights, ones, preferred_element_type=jnp.float32)
                mixed = jnp.dot(weights, all_values[c], preferred_element_type=jnp.float32)
                out_v[c * SPAN : (c + 1) * SPAN, head] = (mixed / total).astype(jnp.bfloat16)
        result(n).start()
        return carry

    def end(n, carry):
        result(n).wait()
        return carry

    lax.fori_loop(0, groups, start, 0)
    lax.fori_loop(0, groups, attend, 0)
    lax.fori_loop(0, groups, end, 0)


def on_device(
    dec_hidden,
    dec_query,
    store,
    norm_gain,
    w_query_enc,
    w_cond,
    w_out_enc,
    w_kv_dec,
    owner,
    nb_index,
    nb_count,
):
    scale = 1.0 / math.sqrt(HEAD)
    n_t = lax.axis_size("tensor")
    tokens = dec_hidden.shape[0]
    spans = tokens // SPAN
    pairs = spans * KN
    rows = pairs * NBLEN
    stored, _, width_e = store.shape
    width_q = w_query_enc.shape[1]
    width_kv = w_kv_dec.shape[1]
    owner_t, index_t = owner.T, nb_index.T
    bf16, f32 = jnp.bfloat16, jnp.float32
    quarter = w_out_enc.shape[0] // 4
    half_c = 2 * HEAD
    anywhere = pl.BlockSpec(memory_space=pl.ANY)
    copies = 2 * 90 + 20 + 8 + 6 + 6
    kv_all, extra = pl.pallas_call(
        functools.partial(exchange_kernel, scale, n_t),
        out_shape=(
            jax.ShapeDtypeStruct((lax.axis_size("dp") * stored, NBLEN, width_kv), bf16),
            jax.ShapeDtypeStruct((rows, width_kv), bf16),
        ),
        in_specs=[
            pl.BlockSpec(memory_space=pltpu.SMEM),
            pl.BlockSpec(memory_space=pltpu.SMEM),
            pl.BlockSpec(memory_space=pltpu.VMEM),
        ]
        + [anywhere] * 6,
        out_specs=(anywhere, anywhere),
        scratch_shapes=[
            pltpu.VMEM((stored, NBLEN, width_e), bf16),
            pltpu.VMEM(w_query_enc.shape, bf16),
            pltpu.VMEM(w_kv_dec.shape, bf16),
            pltpu.VMEM(dec_hidden.shape, bf16),
            pltpu.VMEM(w_cond.shape, bf16),
            pltpu.VMEM((n_t, 2, 2, quarter, width_e), bf16),
            pltpu.VMEM((n_t * w_out_enc.shape[0], width_kv), bf16),
            pltpu.VMEM((stored, NBLEN, width_kv), bf16),
            pltpu.VMEM((lax.axis_size("dp") * stored, NBLEN, width_q), bf16),
            pltpu.VMEM((pairs, NBLEN, width_q), bf16),
            pltpu.VMEM((stored, NBLEN, width_e), bf16),
            pltpu.VMEM((2, tokens, half_c), bf16),
            pltpu.VMEM((2, tokens, half_c), bf16),
            pltpu.VMEM((2, tokens, half_c), bf16),
            pltpu.VMEM((2, tokens, half_c), f32),
            pltpu.VMEM((2, tokens, half_c), bf16),
            pltpu.VMEM((2, tokens, half_c), bf16),
            pltpu.VMEM((2, tokens, half_c), bf16),
            pltpu.VMEM((2, tokens, half_c), bf16),
            pltpu.VMEM((n_t, 2, rows, HEAD), bf16),
            pltpu.SemaphoreType.DMA((copies,)),
            pltpu.SemaphoreType.DMA((copies,)),
            pltpu.SemaphoreType.DMA((9,)),
        ],
        compiler_params=pltpu.CompilerParams(
            collective_id=0, has_side_effects=True, vmem_limit_bytes=60 << 20
        ),
        name="exchange",
    )(
        owner_t,
        index_t,
        norm_gain.reshape(1, width_e),
        store,
        w_query_enc,
        w_kv_dec,
        dec_hidden,
        w_cond,
        w_out_enc.reshape(2, 2, quarter, width_e),
    )

    heads_width = dec_query.shape[1]
    groups = heads_width // (HEADS * HEAD)
    return pl.pallas_call(
        functools.partial(decoder_kernel, scale, stored),
        out_shape=jax.ShapeDtypeStruct((tokens, heads_width), bf16),
        grid_spec=pltpu.PrefetchScalarGridSpec(
            num_scalar_prefetch=3,
            grid=(1,),
            in_specs=[anywhere] * 3,
            out_specs=anywhere,
            scratch_shapes=[
                pltpu.VMEM((pairs, NBLEN, width_kv), bf16),
                pltpu.VMEM((rows, width_kv), bf16),
                pltpu.VMEM((tokens, heads_width), bf16),
                pltpu.VMEM((tokens, heads_width), bf16),
                pltpu.SemaphoreType.DMA((groups, pairs + 2)),
                pltpu.SemaphoreType.DMA((groups,)),
            ],
        ),
        compiler_params=pltpu.CompilerParams(vmem_limit_bytes=56 << 20),
        name="decoder_attention",
    )(owner_t, index_t, nb_count, kv_all, extra, dec_query)


def solution(mesh):
    in_specs = (
        P("dp", "tensor"),
        P("dp", "tensor"),
        P("dp", None, None),
        P(),
        P(None, "tensor"),
        P("tensor", None),
        P("tensor", None),
        P(None, "tensor"),
        P("dp", None),
        P("dp", None),
        P("dp"),
    )
    out_specs = P("dp", "tensor")
    return jax.shard_map(
        on_device, mesh=mesh, in_specs=in_specs, out_specs=out_specs, check_vma=False
    )
```

```python
import functools
import math

import jax
import jax.numpy as jnp
from jax import lax
from jax.experimental import pallas as pl
from jax.experimental.pallas import tpu as pltpu
from jax.sharding import PartitionSpec as P

HEAD = 128
SPAN = 64
NBLEN = 64
KN = 2


MESH = pl.DeviceIdType.MESH
SIDE = 4
CORES = 2
HEADS = 2


class Link:
    def __init__(self, send_sem, recv_sem):
        self.send_sem, self.recv_sem, self.sent, self.drained = send_sem, recv_sem, [], 0

    def send(self, src, dst, device):
        n = len(self.sent)
        copy = pltpu.make_async_remote_copy(
            src_ref=src,
            dst_ref=dst,
            send_sem=self.send_sem.at[n],
            recv_sem=self.recv_sem.at[n],
            device_id=device,
            device_id_type=MESH,
        )
        copy.start()
        self.sent.append(copy)
        return copy

    def drain(self, upto):
        for copy in self.sent[self.drained : upto]:
            copy.wait_send()
        self.drained = upto


class Gather:
    def __init__(self, link, own, out):
        self.link, self.own, self.out = link, own, out
        self.y, self.x, self.k, self.t = place()
        self.copies, self.aside, self.first = {}, [], {}

    def device(self, half, first, second, core=None):
        x, y = (first, second) if half == 0 else (second, first)
        return dp_index(self.x + x, self.y + y, self.k if core is None else core), self.t

    def at(self, half, first, second, item, count):
        x, y = (first, second) if half == 0 else (second, first)
        block = dp_index(self.x + x + SIDE, self.y + y + SIDE, self.k)
        return self.out.at[pl.ds(block * 4 + half * 2 + item, count)]

    def source(self, half, block, item, count):
        if self.own is not None and block == (0, 0):
            return self.own.at[pl.ds(half * 2 + item, count)]
        return self.at(half, *block, item, count)

    def to(self, half, name, block, item, count):
        way = {"P+": (1, 0), "P-": (-1, 0), "S+": (0, 1), "S-": (0, -1)}[name[:2]]
        self.copies[half, name] = self.link.send(
            self.source(half, block, item, count),
            self.at(half, *block, item, count),
            self.device(half, *way),
        )

    def side(self, half, block, item, count):
        self.aside.append(
            self.link.send(
                self.source(half, block, item, count),
                self.at(half, *block, item, count),
                self.device(half, 0, 0, 1 - self.k),
            )
        )

    def got(self, half, name, block, item, count):
        self.copies[half, name].wait_recv()
        self.side(half, block, item, count)

    def start(self, h, item, count):
        for way in ("P+", "P-", "S+", "S-"):
            self.to(h, f"{way} {item}", (0, 0), item, count)
        self.side(h, (0, 0), item, count)
        self.first.setdefault(h, []).append((item, count))

    def arrived(self, h, way, block):
        for item, count in self.first[h]:
            self.got(h, f"{way} {item}", block, item, count)

    def second(self, h):
        self.arrived(h, "P+", (-1, 0))
        self.to(h, "P+f", (-1, 0), 0, 1)
        self.to(h, "S+l", (-1, 0), 0, 2)
        self.to(h, "S-l", (-1, 0), 0, 2)
        self.arrived(h, "P-", (1, 0))
        self.to(h, "P-f", (1, 0), 1, 1)
        self.to(h, "S+r", (1, 0), 0, 2)
        self.to(h, "S-r", (1, 0), 0, 2)
        self.arrived(h, "S+", (0, -1))
        self.to(h, "S+f", (0, -1), 0, 1)
        self.arrived(h, "S-", (0, 1))
        self.to(h, "S-f", (0, 1), 1, 1)

    def third(self, h):
        self.got(h, "P+f", (-2, 0), 0, 1)
        self.to(h, "S+0", (-2, 0), 0, 1)
        self.to(h, "S-0", (-2, 0), 0, 1)
        self.got(h, "P-f", (2, 0), 1, 1)
        self.to(h, "S+1", (2, 0), 1, 1)
        self.to(h, "S-1", (2, 0), 1, 1)
        self.got(h, "S+l", (-1, -1), 0, 2)
        self.to(h, "S+lf", (-1, -1), 0, 1)
        self.got(h, "S-l", (-1, 1), 0, 2)
        self.to(h, "S-lf", (-1, 1), 1, 1)
        self.got(h, "S+r", (1, -1), 0, 2)
        self.to(h, "S+rf", (1, -1), 0, 1)
        self.got(h, "S-r", (1, 1), 0, 2)
        self.to(h, "S-rf", (1, 1), 1, 1)
        self.got(h, "S+f", (0, -2), 0, 1)
        self.got(h, "S-f", (0, 2), 1, 1)

    def fourth(self, h):
        self.got(h, "S+0", (-2, -1), 0, 1)
        self.to(h, "S+0f", (-2, -1), 0, 1)
        self.got(h, "S-1", (2, 1), 1, 1)
        self.to(h, "S-1f", (2, 1), 1, 1)
        self.got(h, "S+1", (2, -1), 1, 1)
        self.got(h, "S-0", (-2, 1), 0, 1)
        self.got(h, "S+lf", (-1, -2), 0, 1)
        self.got(h, "S-lf", (-1, 2), 1, 1)
        self.got(h, "S+rf", (1, -2), 0, 1)
        self.got(h, "S-rf", (1, 2), 1, 1)

    def fifth(self, h):
        self.got(h, "S+0f", (-2, -2), 0, 1)
        self.got(h, "S-1f", (2, 2), 1, 1)

    def finish(self, upto=None):
        for copy in self.aside[:upto]:
            copy.wait_recv()
        self.aside = self.aside[len(self.aside) if upto is None else upto :]


def dp_index(x, y, core):
    return (y % SIDE * SIDE + x % SIDE) * CORES + core


def place():
    me = lax.axis_index("dp")
    return me // (SIDE * CORES), me // CORES % SIDE, me % CORES, lax.axis_index("tensor")


def exchange_kernel(
    scale,
    n_t,
    owner_ref,
    index_ref,
    gain_ref,
    store_ref,
    wq_ref,
    wkv_ref,
    hidden_ref,
    wc_ref,
    wout_ref,
    kv_all_ref,
    c_ref,
    store_v,
    wq_v,
    wkv_v,
    hidden_v,
    wc_v,
    wout_v,
    joined_v,
    kv_own_v,
    q_all_v,
    q_sel_v,
    normed_v,
    far_v,
    up_v,
    down_v,
    own_v,
    far_in_v,
    left_v,
    right_v,
    cond_v,
    ctx_v,
    send_sem,
    recv_sem,
    load_sem,
):
    y, x, core, t = place()
    me = lax.axis_index("dp")
    above, below = (me, (t + 1) % n_t), (me, (t + n_t - 1) % n_t)
    twin = (dp_index(x, y, 1 - core), t)
    stored = store_v.shape[0]
    tile = 2 * HEAD
    tiles = wkv_v.shape[1] // tile
    pairs = q_sel_v.shape[0]
    spans = pairs // KN

    loads = [
        pltpu.make_async_copy(src, dst, load_sem.at[n])
        for n, (src, dst) in enumerate(
            (
                (store_ref, store_v),
                (wq_ref, wq_v),
                (wkv_ref, wkv_v),
                (hidden_ref, hidden_v),
                (wc_ref, wc_v),
                (wout_ref, wout_v.at[0]),
            )
        )
    ]
    for load in loads[:3]:
        load.start()
    barrier = pltpu.get_barrier_semaphore()
    beside = [
        (dp_index(x + 1, y, core), t),
        (dp_index(x + SIDE - 1, y, core), t),
        (dp_index(x, y + 1, core), t),
        (dp_index(x, y + SIDE - 1, core), t),
        twin,
        above,
        below,
    ]
    for device in beside:
        pl.semaphore_signal(barrier, inc=1, device_id=device, device_id_type=MESH)

    link = Link(send_sem, recv_sem)
    q_gather = Gather(link, None, q_all_v)
    kv_gather = Gather(link, kv_own_v, kv_all_ref)

    loads[0].wait()
    gain = gain_ref[...]
    for n in range(stored):
        rows = store_v[n].astype(jnp.float32)
        spread = jnp.mean(rows * rows, axis=-1, keepdims=True)
        normed_v[n] = (rows * lax.rsqrt(spread + 1e-05) * gain).astype(jnp.bfloat16)
    loads[1].wait()
    q_own = (
        jnp.dot(
            normed_v[...].reshape(stored * NBLEN, normed_v.shape[2]),
            wq_v[...],
            preferred_element_type=jnp.float32,
        )
        .astype(jnp.bfloat16)
        .reshape(stored, NBLEN, wq_v.shape[1])
    )
    for half in (0, 1):
        q_gather.at(half, 0, 0, 0, 2)[...] = q_own[2 * half : 2 * half + 2]
    pl.semaphore_wait(barrier, len(beside))
    for half in (0, 1):
        q_gather.start(half, 0, 2)
    w_up = link.send(wout_ref.at[core], wout_v.at[1, core], above)
    w_down = link.send(wout_ref.at[core], wout_v.at[2, core], below)
    loads[2].wait()
    for load in loads[3:]:
        load.start()

    def kv_tile(n, carry):
        columns = pl.ds(pl.multiple_of(n * tile, tile), tile)
        kv_own_v[:, :, columns] = (
            jnp.dot(
                store_v[...].reshape(stored * NBLEN, store_v.shape[2]),
                wkv_v[:, columns],
                preferred_element_type=jnp.float32,
            )
            .astype(jnp.bfloat16)
            .reshape(stored, NBLEN, tile)
        )
        return carry

    lax.fori_loop(0, tiles // 2, kv_tile, 0)
    for half in (0, 1):
        q_gather.second(half)
    lax.fori_loop(tiles // 2, tiles, kv_tile, 0)
    for half in (0, 1):
        q_gather.third(half)
    kv_gather.start(0, 0, 1)
    kv_gather.start(0, 1, 1)
    kept = []
    for half in (0, 1):
        copy = pltpu.make_async_copy(
            kv_own_v.at[pl.ds(2 * half, 2)],
            kv_gather.at(half, 0, 0, 0, 2),
            load_sem.at[len(loads) + half],
        )
        copy.start()
        kept.append(copy)

    loads[3].wait()
    loads[4].wait()

    def part(block, half):
        column = ((t + block) % n_t * 2 + half) * tile
        return jnp.dot(
            hidden_v[...],
            wc_v[:, pl.ds(pl.multiple_of(column, tile), tile)],
            preferred_element_type=jnp.float32,
        )

    far_v[0] = part(2, 0).astype(jnp.bfloat16)
    far_up = link.send(far_v.at[0], far_in_v.at[0], above)
    for half in (0, 1):
        q_gather.fourth(half)
    far_v[1] = part(2, 1).astype(jnp.bfloat16)
    far_down = link.send(far_v.at[1], far_in_v.at[1], below)
    kv_gather.start(1, 0, 1)
    kv_gather.start(1, 1, 1)
    up_v[1] = part(1, 1).astype(jnp.bfloat16)
    near_up = link.send(up_v.at[1], left_v.at[1], above)
    down_v[0] = part(3, 0).astype(jnp.bfloat16)
    near_down = link.send(down_v.at[0], right_v.at[0], below)
    first_up = part(1, 0)
    first_down = part(3, 1)
    own_v[0] = part(0, 0)
    own_v[1] = part(0, 1)
    kv_gather.second(0)
    far_up.wait_recv()
    up_v[0] = (first_up + far_in_v[0].astype(jnp.float32)).astype(jnp.bfloat16)
    last_up = link.send(up_v.at[0], left_v.at[0], above)
    far_down.wait_recv()
    down_v[1] = (first_down + far_in_v[1].astype(jnp.float32)).astype(jnp.bfloat16)
    last_down = link.send(down_v.at[1], right_v.at[1], below)

    w_up.wait_recv()
    w_far_up = link.send(wout_v.at[1, core, 0], wout_v.at[3, core, 0], above)
    w_aside = [link.send(wout_v.at[1, core], wout_v.at[1, core], twin)]
    w_down.wait_recv()
    w_far_down = link.send(wout_v.at[2, core, 1], wout_v.at[3, core, 1], below)
    w_aside.append(link.send(wout_v.at[2, core], wout_v.at[2, core], twin))
    for half in (0, 1):
        q_gather.fifth(half)
    q_gather.finish()

    def pick(c, carry):
        for k in range(KN):
            q_sel_v[KN * c + k] = q_all_v[owner_ref[k, c] * stored + index_ref[k, c]]
        return carry

    lax.fori_loop(0, spans, pick, 0)
    kv_gather.second(1)

    for copy in (near_up, near_down, last_up, last_down):
        copy.wait_recv()
    for h in range(2):
        cond_v[h] = (
            own_v[h] + left_v[h].astype(jnp.float32) + right_v[h].astype(jnp.float32)
        ).astype(jnp.bfloat16)
    for h in range(2):
        query = q_sel_v[:, :, h * HEAD : (h + 1) * HEAD].reshape(spans, KN * NBLEN, HEAD)
        keys = cond_v[h, :, :HEAD].reshape(spans, SPAN, HEAD)
        values = cond_v[h, :, HEAD:].reshape(spans, SPAN, HEAD)
        scores = (
            jnp.einsum("cld,ckd->clk", query, keys, preferred_element_type=jnp.float32) * scale
        )
        weights = jnp.exp(scores - jnp.max(scores, axis=-1, keepdims=True))
        weights = (weights / jnp.sum(weights, axis=-1, keepdims=True)).astype(jnp.bfloat16)
        context = jnp.einsum("clk,ckd->cld", weights, values, preferred_element_type=jnp.float32)
        ctx_v[0, h] = context.astype(jnp.bfloat16).reshape(ctx_v.shape[2], HEAD)
        if h == 0:
            ctx_up = [link.send(ctx_v.at[0, 0], ctx_v.at[1, 0], above)]
    ctx_down = [link.send(ctx_v.at[0, 1], ctx_v.at[2, 1], below)]
    ctx_up.append(link.send(ctx_v.at[0, 1], ctx_v.at[1, 1], above))
    ctx_down.append(link.send(ctx_v.at[0, 0], ctx_v.at[2, 0], below))

    w_far_up.wait_recv()
    w_aside.append(link.send(wout_v.at[3, core, 0], wout_v.at[3, core, 0], twin))
    w_far_down.wait_recv()
    w_aside.append(link.send(wout_v.at[3, core, 1], wout_v.at[3, core, 1], twin))
    loads[5].wait()
    for copy in w_aside:
        copy.wait_recv()

    def joined_tile(n, carry):
        columns = pl.ds(pl.multiple_of(n * tile, tile), tile)
        joined_v[:, columns] = jnp.dot(
            wout_v[...].reshape(joined_v.shape[0], wout_v.shape[4]),
            wkv_v[:, columns],
            preferred_element_type=jnp.float32,
        ).astype(jnp.bfloat16)
        return carry

    lax.fori_loop(0, tiles, joined_tile, 0)

    ctx_up[0].wait_recv()
    ctx_far_up = link.send(ctx_v.at[1, 0], ctx_v.at[3, 0], above)
    ctx_down[0].wait_recv()
    ctx_far_down = link.send(ctx_v.at[2, 1], ctx_v.at[3, 1], below)

    early, handed = len(link.sent), len(kv_gather.aside)
    kv_gather.third(0)
    ctx_up[1].wait_recv()
    ctx_down[1].wait_recv()
    rows = ctx_v.shape[2]

    def term(j, columns):
        return jnp.dot(
            jnp.concatenate([ctx_v[j, 0], ctx_v[j, 1]], axis=-1),
            joined_v[j * 2 * HEAD : (j + 1) * 2 * HEAD, columns],
            preferred_element_type=jnp.float32,
        )

    def c_near(n, carry):
        columns = pl.ds(pl.multiple_of(n * tile, tile), tile)
        total = term(0, columns) + term(1, columns) + term(2, columns)
        wc_v[:rows, columns] = total.astype(jnp.bfloat16)
        return carry

    def c_far(n, carry):
        columns = pl.ds(pl.multiple_of(n * tile, tile), tile)
        total = wc_v[:rows, columns].astype(jnp.float32) + term(3, columns)
        wc_v[:rows, columns] = total.astype(jnp.bfloat16)
        return carry

    lax.fori_loop(0, tiles // 2, c_near, 0)
    kv_gather.third(1)
    lax.fori_loop(tiles // 2, tiles, c_near, 0)
    ctx_far_up.wait_recv()
    ctx_far_down.wait_recv()
    lax.fori_loop(0, tiles, c_far, 0)
    out = pltpu.make_async_copy(wc_v.at[pl.ds(0, rows)], c_ref, load_sem.at[len(loads) + 2])
    out.start()
    late = len(link.sent)
    for half in (0, 1):
        kv_gather.fourth(half)
    link.drain(early)
    kv_gather.finish(handed)
    out.wait()
    for copy in kept:
        copy.wait()
    for half in (0, 1):
        kv_gather.fifth(half)
    link.drain(late)
    kv_gather.finish()
    link.drain(len(link.sent))


def decoder_kernel(
    scale,
    stored,
    owner_ref,
    index_ref,
    count_ref,
    kv_ref,
    c_ref,
    q_ref,
    out_ref,
    kv_v,
    c_v,
    q_v,
    out_v,
    in_sem,
    out_sem,
):
    pairs = kv_v.shape[0]
    spans = pairs // KN
    groups = in_sem.shape[0]
    width = HEADS * HEAD
    key_place = lax.broadcasted_iota(jnp.int32, (SPAN, KN * NBLEN), 1) // NBLEN
    ones = jnp.ones((KN * NBLEN, HEAD), jnp.bfloat16)

    def part(n, size):
        return pl.ds(pl.multiple_of(n * size, size), size)

    def fetches(n):
        wide, narrow = part(n, 2 * width), part(n, width)
        copies = []
        for p in range(pairs):
            row = owner_ref[p % KN, p // KN] * stored + index_ref[p % KN, p // KN]
            copies.append(
                pltpu.make_async_copy(
                    kv_ref.at[row, :, wide], kv_v.at[p, :, wide], in_sem.at[n, p]
                )
            )
        copies.append(
            pltpu.make_async_copy(c_ref.at[:, wide], c_v.at[:, wide], in_sem.at[n, pairs])
        )
        copies.append(
            pltpu.make_async_copy(q_ref.at[:, narrow], q_v.at[:, narrow], in_sem.at[n, pairs + 1])
        )
        return copies

    def result(n):
        narrow = part(n, width)
        return pltpu.make_async_copy(out_v.at[:, narrow], out_ref.at[:, narrow], out_sem.at[n])

    def start(n, carry):
        for copy in fetches(n):
            copy.start()
        return carry

    def attend(n, carry):
        for copy in fetches(n):
            copy.wait()
        for g in range(HEADS):
            columns, head = part(n * HEADS + g, 2 * HEAD), part(n * HEADS + g, HEAD)
            all_scores = []
            all_values = []
            for c in range(spans):
                stored_kv = kv_v[KN * c : KN * (c + 1), :, columns].reshape(KN * NBLEN, 2 * HEAD)
                here = c_v[c * KN * NBLEN : (c + 1) * KN * NBLEN, columns] + stored_kv
                all_values.append(here[:, HEAD:])
                scores = (
                    lax.dot_general(
                        q_v[c * SPAN : (c + 1) * SPAN, head],
                        here[:, :HEAD],
                        (((1,), (1,)), ((), ())),
                        preferred_element_type=jnp.float32,
                    )
                    * scale
                )
                all_scores.append(jnp.where(key_place < count_ref[c], scores, jnp.float32(-1e30)))
            for c in range(spans):
                scores = all_scores[c]
                weights = jnp.exp(scores - jnp.max(scores, axis=-1, keepdims=True)).astype(
                    jnp.bfloat16
                )
                total = jnp.dot(weights, ones, preferred_element_type=jnp.float32)
                mixed = jnp.dot(weights, all_values[c], preferred_element_type=jnp.float32)
                out_v[c * SPAN : (c + 1) * SPAN, head] = (mixed / total).astype(jnp.bfloat16)
        result(n).start()
        return carry

    def end(n, carry):
        result(n).wait()
        return carry

    lax.fori_loop(0, groups, start, 0)
    lax.fori_loop(0, groups, attend, 0)
    lax.fori_loop(0, groups, end, 0)


def on_device(
    dec_hidden,
    dec_query,
    store,
    norm_gain,
    w_query_enc,
    w_cond,
    w_out_enc,
    w_kv_dec,
    owner,
    nb_index,
    nb_count,
):
    scale = 1.0 / math.sqrt(HEAD)
    n_t = lax.axis_size("tensor")
    tokens = dec_hidden.shape[0]
    spans = tokens // SPAN
    pairs = spans * KN
    rows = pairs * NBLEN
    stored, _, width_e = store.shape
    width_q = w_query_enc.shape[1]
    width_kv = w_kv_dec.shape[1]
    owner_t, index_t = owner.T, nb_index.T
    bf16, f32 = jnp.bfloat16, jnp.float32
    quarter = w_out_enc.shape[0] // 4
    half_c = 2 * HEAD
    anywhere = pl.BlockSpec(memory_space=pl.ANY)
    copies = 2 * 90 + 20 + 8 + 6 + 6
    kv_all, extra = pl.pallas_call(
        functools.partial(exchange_kernel, scale, n_t),
        out_shape=(
            jax.ShapeDtypeStruct((lax.axis_size("dp") * stored, NBLEN, width_kv), bf16),
            jax.ShapeDtypeStruct((rows, width_kv), bf16),
        ),
        in_specs=[
            pl.BlockSpec(memory_space=pltpu.SMEM),
            pl.BlockSpec(memory_space=pltpu.SMEM),
            pl.BlockSpec(memory_space=pltpu.VMEM),
        ]
        + [anywhere] * 6,
        out_specs=(anywhere, anywhere),
        scratch_shapes=[
            pltpu.VMEM((stored, NBLEN, width_e), bf16),
            pltpu.VMEM(w_query_enc.shape, bf16),
            pltpu.VMEM(w_kv_dec.shape, bf16),
            pltpu.VMEM(dec_hidden.shape, bf16),
            pltpu.VMEM(w_cond.shape, bf16),
            pltpu.VMEM((n_t, 2, 2, quarter, width_e), bf16),
            pltpu.VMEM((n_t * w_out_enc.shape[0], width_kv), bf16),
            pltpu.VMEM((stored, NBLEN, width_kv), bf16),
            pltpu.VMEM((lax.axis_size("dp") * stored, NBLEN, width_q), bf16),
            pltpu.VMEM((pairs, NBLEN, width_q), bf16),
            pltpu.VMEM((stored, NBLEN, width_e), bf16),
            pltpu.VMEM((2, tokens, half_c), bf16),
            pltpu.VMEM((2, tokens, half_c), bf16),
            pltpu.VMEM((2, tokens, half_c), bf16),
            pltpu.VMEM((2, tokens, half_c), f32),
            pltpu.VMEM((2, tokens, half_c), bf16),
            pltpu.VMEM((2, tokens, half_c), bf16),
            pltpu.VMEM((2, tokens, half_c), bf16),
            pltpu.VMEM((2, tokens, half_c), bf16),
            pltpu.VMEM((n_t, 2, rows, HEAD), bf16),
            pltpu.SemaphoreType.DMA((copies,)),
            pltpu.SemaphoreType.DMA((copies,)),
            pltpu.SemaphoreType.DMA((9,)),
        ],
        compiler_params=pltpu.CompilerParams(
            collective_id=0, has_side_effects=True, vmem_limit_bytes=60 << 20
        ),
        name="exchange",
    )(
        owner_t,
        index_t,
        norm_gain.reshape(1, width_e),
        store,
        w_query_enc,
        w_kv_dec,
        dec_hidden,
        w_cond,
        w_out_enc.reshape(2, 2, quarter, width_e),
    )

    heads_width = dec_query.shape[1]
    groups = heads_width // (HEADS * HEAD)
    return pl.pallas_call(
        functools.partial(decoder_kernel, scale, stored),
        out_shape=jax.ShapeDtypeStruct((tokens, heads_width), bf16),
        grid_spec=pltpu.PrefetchScalarGridSpec(
            num_scalar_prefetch=3,
            grid=(1,),
            in_specs=[anywhere] * 3,
            out_specs=anywhere,
            scratch_shapes=[
                pltpu.VMEM((pairs, NBLEN, width_kv), bf16),
                pltpu.VMEM((rows, width_kv), bf16),
                pltpu.VMEM((tokens, heads_width), bf16),
                pltpu.VMEM((tokens, heads_width), bf16),
                pltpu.SemaphoreType.DMA((groups, pairs + 2)),
                pltpu.SemaphoreType.DMA((groups,)),
            ],
        ),
        compiler_params=pltpu.CompilerParams(vmem_limit_bytes=56 << 20),
        name="decoder_attention",
    )(owner_t, index_t, nb_count, kv_all, extra, dec_query)


def solution(mesh):
    in_specs = (
        P("dp", "tensor"),
        P("dp", "tensor"),
        P("dp", None, None),
        P(),
        P(None, "tensor"),
        P("tensor", None),
        P("tensor", None),
        P(None, "tensor"),
        P("dp", None),
        P("dp", None),
        P("dp"),
    )
    out_specs = P("dp", "tensor")
    return jax.shard_map(
        on_device, mesh=mesh, in_specs=in_specs, out_specs=out_specs, check_vma=False
    )
```
